512 devices in a mesh: au: 32 (over z, y_lo), ia: 16 (over x, y_hi, core).
Axes of the slice: x: 4, y: 8 (y_hi: 2, y_lo: 4; y = y_hi * 4 + y_lo), z: 8, core: 2. Of those that a mesh axis runs over, the one named last changes fastest.
Arguments:
- user_emb: bfloat16 [32, 2048, 256], P('au', 'ia'), may hold values from -6 to 6
- item_emb: bfloat16 [16, 1024, 256], P('ia', 'au'), may hold values from -6 to 6
- weight: bfloat16 [256, 256], replicated, may hold values from -0.375 to 0.375
- grad_user: bfloat16 [32, 2048, 256], P('au', 'ia'), may hold values from -6 to 6
- grad_item: bfloat16 [16, 1024, 256], P('ia', 'au'), may hold values from -6 to 6
- tile_values: bfloat16 [32, 2048, 128, 128], P('au', 'ia'), may hold values from 0 to 1
- tile_rows: int32 [32, 2048], P('au', 'ia'), may hold values from 0 to 15
- tile_cols: int32 [32, 2048], P('au', 'ia'), may hold values from 0 to 7
- tile_norm: int32 [32, 2048], P('au', 'ia'), may hold values from 32 to 128
- tile_count: int32 [32, 16], P('au', 'ia'), may hold values from 64 to 128, as said below
Outputs:
- grad_user_emb: bfloat16 [32, 2048, 256], P('au', 'ia')
- grad_item_emb: bfloat16 [16, 1024, 256], P('ia', 'au')
- grad_weight: float32 [256, 256], replicated
The draws below stay inside these ranges and needn't reach their ends.
Inputs may be any that keep to these rules, and one draw needn't show every extreme that they name: `tile_rows`: slots of one block pair may name the same tile position; their terms add. Slots at and after tile_count[a, b] are unused; some block pair has exactly 128 live slots in every draw.
All inputs are finite; a program needn't handle non-finite values.
Results may differ from the reference program's by a relative error of at most 0.025.
Values may be sent and summed in bfloat16 or wider, within the bound.
No kernel may reach another device: no remote copies, remote signals or barrier semaphores. Data moves between devices by JAX's collectives and lax.ppermute only.
A program may use at most 64 MiB of HBM per device.

```python
import math
import jax
import jax.numpy as jnp
from jax import lax

D = 256
TILE = 128
UT = 16
IT = 8
CAP = 128
USERS = 65536
ITEMS = 16384
N_AU = 32
N_IA = 16


def draw_tile_count(key, part):
    low_key, pick_key = jax.random.split(jax.random.fold_in(key, 7))
    counts = jax.random.randint(low_key, (N_AU * N_IA,), CAP // 2, CAP + 1)
    chosen = jax.random.randint(pick_key, (), 0, N_AU * N_IA)
    flattened = jnp.where(jnp.arange(N_AU * N_IA) == chosen, CAP, counts)
    return flattened.reshape(N_AU, N_IA).astype(jnp.int32)


def set_ends(values, stream_key, least, largest):
    longest = values.shape.index(max(values.shape))
    spots = []
    for shift in (0, 1):
        where = [jax.random.randint(jax.random.fold_in(stream_key, axis), (), 0, length) for axis, length in enumerate(values.shape)]
        where[longest] = (where[longest] + shift) % values.shape[longest]
        spots.append(tuple(where))
    return values.at[spots[0]].set(least).at[spots[1]].set(largest)


def level_of(stream_key, dims, pieces, least, top_value):
    level = 1.0
    for position, blocks in pieces:
        heights = jax.random.uniform(jax.random.fold_in(jax.random.fold_in(stream_key, 6), position), (blocks,), jnp.float32, least / len(pieces), top_value / len(pieces))
        level = level * jnp.repeat(jnp.exp(heights), dims[position] // blocks).reshape((-1,) + (1,) * (len(dims) - 1 - position))
    return level


def bell_draw(rng, extent, width, reach, cuts=(), kind=jnp.bfloat16):
    level = level_of(rng, extent, cuts, -0.22, 0.18) if cuts else 1.0
    values = jax.random.normal(rng, extent, jnp.float32) * width * level
    return jnp.minimum(jnp.maximum(values, -reach), reach).astype(kind)


def setup_inputs(seed: int = 0) -> dict:
    key_of = jax.random.split(jax.random.key(seed), 11)
    user_emb = bell_draw(key_of[0], (N_AU, UT * TILE, D), 1.0, 6.0, ((0, 32), (1, 16)))
    item_emb = bell_draw(key_of[1], (N_IA, IT * TILE, D), 1.0, 6.0, ((0, 16), (1, 32)))
    weight = bell_draw(key_of[2], (D, D), D ** -0.5, 0.375)
    grad_user = bell_draw(key_of[3], (N_AU, UT * TILE, D), 1.0, 6.0, ((0, 32), (1, 16)))
    grad_item = bell_draw(key_of[4], (N_IA, IT * TILE, D), 1.0, 6.0, ((0, 16), (1, 32)))
    tile_values = jnp.clip(1.0 * jax.random.uniform(key_of[5], (N_AU, N_IA * CAP, TILE, TILE), jnp.float32) ** level_of(key_of[5], (N_AU, N_IA * CAP, TILE, TILE), ((0, 32), (1, 16)), -0.2, 0.2), 0.0, 1.0).astype(jnp.bfloat16)
    tile_rows = set_ends(jax.random.randint(key_of[6], (N_AU, N_IA * CAP), 0, UT), jax.random.fold_in(key_of[6], 1), 0, UT - 1).astype(jnp.int32)
    tile_cols = set_ends(jax.random.randint(key_of[7], (N_AU, N_IA * CAP), 0, IT), jax.random.fold_in(key_of[7], 1), 0, IT - 1).astype(jnp.int32)
    tile_norm = set_ends(jax.random.randint(key_of[8], (N_AU, N_IA * CAP), 32, 129), jax.random.fold_in(key_of[8], 1), 32, 128).astype(jnp.int32)
    tile_count = draw_tile_count(jax.random.fold_in(key_of[10], 71), 0)
    return {"user_emb": user_emb, "item_emb": item_emb, "weight": weight, "grad_user": grad_user, "grad_item": grad_item, "tile_values": tile_values, "tile_rows": tile_rows, "tile_cols": tile_cols, "tile_norm": tile_norm, "tile_count": tile_count}


slot_group = 8

def rounded(value):
    return lax.optimization_barrier(value.astype(jnp.bfloat16)).astype(jnp.float32)

def device_terms(tile_block, row_ids, col_ids, norm_ids, live_count, item_source, user_source):
    turn_count = (live_count + slot_group - 1) // slot_group

    def one_turn(turn_index, totals):
        user_total, item_total = totals
        first_slot = (turn_index * slot_group).astype(jnp.int32)
        values = lax.dynamic_slice_in_dim(tile_block, first_slot, slot_group, 0).astype(jnp.float32)
        row_pick = lax.dynamic_slice_in_dim(row_ids, first_slot, slot_group, 0)
        col_pick = lax.dynamic_slice_in_dim(col_ids, first_slot, slot_group, 0)
        norm_pick = lax.dynamic_slice_in_dim(norm_ids, first_slot, slot_group, 0)
        live_mask = first_slot + jnp.arange(slot_group, dtype=jnp.int32) < live_count
        inverse = jnp.where(live_mask, 1.0 / norm_pick.astype(jnp.float32), 0.0)[:, None, None]
        forward = jnp.einsum('gic,gcd->gid', values, item_source[col_pick].astype(jnp.float32))
        user_total = user_total.at[row_pick].add(forward * inverse)
        backward = jnp.einsum('gic,gid->gcd', values, user_source[row_pick].astype(jnp.float32))
        item_total = item_total.at[col_pick].add(backward * inverse)
        return (user_total, item_total)
    start = (jnp.zeros(user_source.shape, jnp.float32), jnp.zeros(item_source.shape, jnp.float32))
    return lax.fori_loop(jnp.int32(0), turn_count.astype(jnp.int32), one_turn, start)

def reference(user_emb, item_emb, weight, grad_user, grad_item, tile_values, tile_rows, tile_cols, tile_norm, tile_count):

    def per_user_block(item_sum, block_index):
        user_source = grad_user[block_index].reshape(UT, TILE, D)
        block_values = tile_values[block_index]
        block_rows = tile_rows[block_index]
        block_cols = tile_cols[block_index]
        block_norms = tile_norm[block_index]

        def per_item_block(carry, item_index):
            user_total, item_sum = carry
            item_source = grad_item[item_index].reshape(IT, TILE, D)
            slot_start = (item_index * CAP).astype(jnp.int32)
            part_user, part_item = device_terms(lax.dynamic_slice_in_dim(block_values, slot_start, CAP, 0), lax.dynamic_slice_in_dim(block_rows, slot_start, CAP, 0), lax.dynamic_slice_in_dim(block_cols, slot_start, CAP, 0), lax.dynamic_slice_in_dim(block_norms, slot_start, CAP, 0), tile_count[block_index, item_index], item_source, user_source)
            current = lax.dynamic_index_in_dim(item_sum, item_index, 0, keepdims=False)
            item_sum = lax.dynamic_update_index_in_dim(item_sum, current + rounded(part_item).reshape(IT * TILE, D), item_index, 0)
            return ((user_total + rounded(part_user), item_sum), None)
        start = (jnp.zeros((UT, TILE, D), jnp.float32), item_sum)
        (user_total, item_sum), unused = lax.scan(per_item_block, start, jnp.arange(N_IA, dtype=jnp.int32))
        return (item_sum, user_total.reshape(UT * TILE, D))
    q_item, q_user = lax.scan(per_user_block, jnp.zeros((N_IA, IT * TILE, D), jnp.float32), jnp.arange(N_AU, dtype=jnp.int32))
    q_user_low = rounded(q_user)
    q_item_low = rounded(q_item)
    weight_wide = weight.astype(jnp.float32)
    grad_user_emb = jnp.einsum('bre,de->brd', q_user_low, weight_wide).astype(jnp.bfloat16)
    grad_item_emb = jnp.einsum('bre,de->brd', q_item_low, weight_wide).astype(jnp.bfloat16)
    user_term = jnp.einsum('brd,bre->de', user_emb.astype(jnp.float32), q_user, precision=lax.Precision.HIGHEST)
    item_term = jnp.einsum('brd,bre->de', item_emb.astype(jnp.float32), q_item, precision=lax.Precision.HIGHEST)
    grad_weight = (user_term + item_term) / math.sqrt(USERS + ITEMS)
    return (grad_user_emb, grad_item_emb, grad_weight)
```

```python
import math

import jax
import jax.numpy as jnp
from jax import lax
from jax.experimental import pallas as pl
from jax.experimental.pallas import tpu as pltpu
from jax.sharding import PartitionSpec as P

slot_block = 16
unroll = 4


def from_everyone(value, axis):
    copies = jnp.broadcast_to(value, (lax.axis_size(axis), *value.shape))
    return lax.all_to_all(copies, axis, split_axis=0, concat_axis=0, tiled=True)


def to_owners(value, axis):
    peers = lax.axis_size(axis)
    pieces = value.reshape(peers, value.shape[0] // peers, *value.shape[1:])
    return lax.all_to_all(pieces, axis, split_axis=0, concat_axis=0, tiled=True)


def summed(pieces):
    return pieces.astype(jnp.float32).sum(axis=0)


def dense_kernel(rows, cols, norms, count, tiles, dense, total):
    step = pl.program_id(0)
    edge = tiles.shape[1]
    user_tiles = dense.shape[0] // edge
    item_tiles = dense.shape[1] // edge

    @pl.when(step == 0)
    def clear():
        def clear_one(index, carry):
            total[index] = jnp.zeros((edge, edge), jnp.float32)
            return carry

        lax.fori_loop(0, total.shape[0], clear_one, 0)

    first = step * slot_block
    live = jnp.clip(count[0] - first, 0, slot_block)

    def add_group(group, carry):
        for lane in range(unroll):
            local = group * unroll + lane
            slot = first + local
            place = rows[slot] * item_tiles + cols[slot]
            norm = jnp.full((8, edge), norms[slot], jnp.int32).astype(jnp.float32)
            scale = jnp.where(slot < count[0], 1.0 / norm, 0.0)
            term = tiles[local].astype(jnp.float32).reshape(edge // 8, 8, edge) * scale[None]
            total[place] = total[place] + term.reshape(edge, edge)
        return carry

    lax.fori_loop(0, (live + unroll - 1) // unroll, add_group, 0)

    @pl.when(step == pl.num_programs(0) - 1)
    def finish():
        def finish_row(row, carry):
            start = pl.multiple_of(row * edge, edge)
            for col in range(item_tiles):
                dense[pl.ds(start, edge), col * edge : (col + 1) * edge] = total[
                    row * item_tiles + col
                ].astype(jnp.bfloat16)
            return carry

        lax.fori_loop(0, user_tiles, finish_row, 0)


def dense_block(tile_block, row_ids, col_ids, norm_ids, count, user_rows, item_rows):
    slots, edge, _ = tile_block.shape
    positions = (user_rows // edge) * (item_rows // edge)
    return pl.pallas_call(
        dense_kernel,
        out_shape=jax.ShapeDtypeStruct((user_rows, item_rows), jnp.bfloat16),
        grid_spec=pltpu.PrefetchScalarGridSpec(
            num_scalar_prefetch=4,
            grid=(slots // slot_block,),
            in_specs=[pl.BlockSpec((slot_block, edge, edge), lambda i, *_: (i, 0, 0))],
            out_specs=pl.BlockSpec((user_rows, item_rows), lambda i, *_: (0, 0)),
            scratch_shapes=[pltpu.VMEM((positions, edge, edge), jnp.float32)],
        ),
        compiler_params=pltpu.CompilerParams(
            dimension_semantics=("arbitrary",), vmem_limit_bytes=40 << 20
        ),
        cost_estimate=pl.CostEstimate(
            flops=4 * slots * edge * edge,
            bytes_accessed=2 * slots * edge * edge + 2 * user_rows * item_rows,
            transcendentals=0,
        ),
        name="dense_block",
    )(row_ids, col_ids, norm_ids, count, tile_block)


def block_product(embedded, total):
    return jnp.einsum(
        "rd,re->de", embedded.astype(jnp.float32), total, precision=lax.Precision.HIGHEST
    )


def per_device(
    user_emb,
    item_emb,
    weight,
    grad_user,
    grad_item,
    tile_values,
    tile_rows,
    tile_cols,
    tile_norm,
    tile_count,
):
    width = weight.shape[0]
    user_rows = user_emb.shape[1] * lax.axis_size("ia")
    item_rows = item_emb.shape[1] * lax.axis_size("au")
    low = jnp.bfloat16
    users = from_everyone(grad_user[0], "ia").reshape(user_rows, width)
    items = from_everyone(grad_item[0], "au").reshape(item_rows, width)
    dense = dense_block(
        tile_values[0],
        tile_rows[0],
        tile_cols[0],
        tile_norm[0],
        tile_count[0],
        user_rows,
        item_rows,
    )
    user_part = jnp.einsum("ui,id->ud", dense, items, preferred_element_type=jnp.float32)
    item_part = jnp.einsum("ui,ud->id", dense, users, preferred_element_type=jnp.float32)
    q_user = summed(to_owners(user_part.astype(low), "ia"))
    q_item = summed(to_owners(item_part.astype(low), "au"))
    weight_part = block_product(user_emb[0], q_user) + block_product(item_emb[0], q_item)
    strip = summed(to_owners(weight_part.astype(low), "ia"))
    strip = summed(from_everyone(strip.astype(low), "au"))
    user_count = user_rows * lax.axis_size("au")
    item_count = item_rows * lax.axis_size("ia")
    strip = strip / math.sqrt(user_count + item_count)
    grad_weight = from_everyone(strip, "ia").reshape(width, width)
    grad_user_emb = jnp.einsum(
        "re,de->rd", q_user.astype(low), weight, preferred_element_type=jnp.float32
    ).astype(low)
    grad_item_emb = jnp.einsum(
        "re,de->rd", q_item.astype(low), weight, preferred_element_type=jnp.float32
    ).astype(low)
    return (grad_user_emb[None], grad_item_emb[None], grad_weight)


def solution(mesh):
    return jax.shard_map(
        per_device,
        mesh=mesh,
        in_specs=(
            P("au", "ia", None),
            P("ia", "au", None),
            P(),
            P("au", "ia", None),
            P("ia", "au", None),
            P("au", "ia", None, None),
            P("au", "ia"),
            P("au", "ia"),
            P("au", "ia"),
            P("au", "ia"),
        ),
        out_specs=(P("au", "ia", None), P("ia", "au", None), P()),
        check_vma=False,
    )
```

```python
import math

import jax
import jax.numpy as jnp
from jax import lax
from jax.experimental import pallas as pl
from jax.experimental.pallas import tpu as pltpu
from jax.sharding import PartitionSpec as P

slot_block = 16
unroll = 4
core_bit = 1
side_bit = 2
ring_step = 4


def from_everyone(value, axis):
    copies = jnp.broadcast_to(value, (lax.axis_size(axis), *value.shape))
    return lax.all_to_all(copies, axis, split_axis=0, concat_axis=0, tiled=True)


def to_owners(value, axis):
    peers = lax.axis_size(axis)
    pieces = value.reshape(peers, value.shape[0] // peers, *value.shape[1:])
    return lax.all_to_all(pieces, axis, split_axis=0, concat_axis=0, tiled=True)


def partner(value, bit):
    return lax.ppermute(value, "ia", [(i, i ^ bit) for i in range(lax.axis_size("ia"))])


def ahead(index, distance):
    ring = lax.axis_size("ia") // ring_step
    return (index // ring_step + distance) % ring * ring_step + index % ring_step


def from_ahead(value, distance):
    size = lax.axis_size("ia")
    return lax.ppermute(value, "ia", [(ahead(i, distance), i) for i in range(size)])


def send_ahead(value, distance):
    size = lax.axis_size("ia")
    return lax.ppermute(value, "ia", [(i, ahead(i, distance)) for i in range(size)])


def relative_rows(row_ids):
    ring = lax.axis_size("ia") // ring_step
    here = lax.axis_index("ia").astype(jnp.int32)
    core = (row_ids ^ here) & 1
    side = ((row_ids ^ here) >> 1) & 1
    along = ((row_ids >> 2) - (here >> 2)) & (ring - 1)
    return core * (2 * ring) + along * 2 + side


def summed(pieces):
    return pieces.astype(jnp.float32).sum(axis=0)


def dense_kernel(rows, cols, norms, count, tiles, near, far, total):
    step = pl.program_id(0)
    edge = tiles.shape[1]
    half_tiles = near.shape[0] // edge
    item_tiles = near.shape[1] // edge

    @pl.when(step == 0)
    def clear():
        def clear_one(index, carry):
            total[index] = jnp.zeros((edge, edge), jnp.float32)
            return carry

        lax.fori_loop(0, total.shape[0], clear_one, 0)

    first = step * slot_block
    live = jnp.clip(count[0] - first, 0, slot_block)

    def add_group(group, carry):
        for lane in range(unroll):
            local = group * unroll + lane
            slot = first + local
            place = rows[slot] * item_tiles + cols[slot]
            norm = jnp.full((8, edge), norms[slot], jnp.int32).astype(jnp.float32)
            scale = jnp.where(slot < count[0], 1.0 / norm, 0.0)
            term = tiles[local].astype(jnp.float32).reshape(edge // 8, 8, edge) * scale[None]
            total[place] = total[place] + term.reshape(edge, edge)
        return carry

    lax.fori_loop(0, (live + unroll - 1) // unroll, add_group, 0)

    @pl.when(step == pl.num_programs(0) - 1)
    def finish():
        def finish_row(row, carry):
            start = pl.multiple_of(row * edge, edge)
            for half, dense in enumerate((near, far)):
                for col in range(item_tiles):
                    place = (half * half_tiles + row) * item_tiles + col
                    dense[pl.ds(start, edge), col * edge : (col + 1) * edge] = total[
                        place
                    ].astype(jnp.bfloat16)
            return carry

        lax.fori_loop(0, half_tiles, finish_row, 0)


def dense_block(tile_block, row_ids, col_ids, norm_ids, count, user_rows, item_rows):
    slots, edge, _ = tile_block.shape
    positions = (user_rows // edge) * (item_rows // edge)
    return pl.pallas_call(
        dense_kernel,
        out_shape=[jax.ShapeDtypeStruct((user_rows // 2, item_rows), jnp.bfloat16)] * 2,
        grid_spec=pltpu.PrefetchScalarGridSpec(
            num_scalar_prefetch=4,
            grid=(slots // slot_block,),
            in_specs=[pl.BlockSpec((slot_block, edge, edge), lambda i, *_: (i, 0, 0))],
            out_specs=[pl.BlockSpec((user_rows // 2, item_rows), lambda i, *_: (0, 0))] * 2,
            scratch_shapes=[pltpu.VMEM((positions, edge, edge), jnp.float32)],
        ),
        compiler_params=pltpu.CompilerParams(
            dimension_semantics=("arbitrary",), vmem_limit_bytes=40 << 20
        ),
        cost_estimate=pl.CostEstimate(
            flops=4 * slots * edge * edge,
            bytes_accessed=2 * slots * edge * edge + 2 * user_rows * item_rows,
            transcendentals=0,
        ),
        name="dense_block",
    )(row_ids, col_ids, norm_ids, count, tile_block)


def product(spec, left, right):
    return jnp.einsum(spec, left, right, preferred_element_type=jnp.float32)


def wide(value):
    return value.astype(jnp.float32)


def per_device(
    user_emb,
    item_emb,
    weight,
    grad_user,
    grad_item,
    tile_values,
    tile_rows,
    tile_cols,
    tile_norm,
    tile_count,
):
    width = weight.shape[0]
    user_rows = user_emb.shape[1] * lax.axis_size("ia")
    item_rows = item_emb.shape[1] * lax.axis_size("au")
    low = jnp.bfloat16
    ring = lax.axis_size("ia") // ring_step

    mine = jnp.stack([grad_user[0], user_emb[0]])
    pair = jnp.stack([mine, partner(mine, side_bit)], axis=1)
    near = jnp.concatenate([pair] + [from_ahead(pair, d) for d in range(1, ring)], axis=1)
    near = near.reshape(2, user_rows // 2, width)
    far = partner(near, core_bit)

    item_pieces = from_everyone(jnp.stack([grad_item[0], item_emb[0]]), "au")
    items = item_pieces[:, 0].reshape(item_rows, width)
    item_table = item_pieces[:, 1].reshape(item_rows, width)

    dense_near, dense_far = dense_block(
        tile_values[0],
        relative_rows(tile_rows[0]),
        tile_cols[0],
        tile_norm[0],
        tile_count[0],
        user_rows,
        item_rows,
    )
    user_far = product("ui,id->ud", dense_far, items).astype(low)
    user_near = product("ui,id->ud", dense_near, items).astype(low)
    item_part = product("ui,ud->id", dense_near, near[0]) + product(
        "ui,ud->id", dense_far, far[0]
    )
    item_part = item_part.astype(low)
    weight_part = (
        product("rd,re->de", near[1], user_near)
        + product("rd,re->de", far[1], user_far)
        + product("rd,re->de", item_table, item_part)
    )

    peers = lax.axis_size("au")
    pieces = jnp.concatenate(
        [
            item_part.reshape(peers, item_rows // peers, width),
            weight_part.astype(low).reshape(peers, width // peers, width),
        ],
        axis=1,
    )
    arrived = summed(lax.all_to_all(pieces, "au", split_axis=0, concat_axis=0, tiled=True))
    q_item = arrived[: item_rows // peers]
    strip = summed(from_everyone(arrived[item_rows // peers :].astype(low), "ia"))
    user_count = user_rows * lax.axis_size("au")
    item_count = item_rows * lax.axis_size("ia")
    strip = strip / math.sqrt(user_count + item_count)
    grad_weight = wide(from_everyone(strip.astype(low), "au")).reshape(width, width)

    along = wide(user_near) + wide(partner(user_far, core_bit))
    along = along.reshape(ring, user_rows // (2 * ring), width)
    sent = along.astype(low)
    both = along[0] + sum(wide(send_ahead(sent[d], d)) for d in range(1, ring))
    own_rows = user_emb.shape[1]
    q_user = both[:own_rows] + wide(partner(both[own_rows:].astype(low), side_bit))

    grad_user_emb = product("re,de->rd", q_user.astype(low), weight).astype(low)
    grad_item_emb = product("re,de->rd", q_item.astype(low), weight).astype(low)
    return (grad_user_emb[None], grad_item_emb[None], grad_weight)


def solution(mesh):
    return jax.shard_map(
        per_device,
        mesh=mesh,
        in_specs=(
            P("au", "ia", None),
            P("ia", "au", None),
            P(),
            P("au", "ia", None),
            P("ia", "au", None),
            P("au", "ia", None, None),
            P("au", "ia"),
            P("au", "ia"),
            P("au", "ia"),
            P("au", "ia"),
        ),
        out_specs=(P("au", "ia", None), P("ia", "au", None), P()),
        check_vma=False,
    )
```

```python
import math

import jax
import jax.numpy as jnp
from jax import lax
from jax.experimental import pallas as pl
from jax.experimental.pallas import tpu as pltpu
from jax.sharding import PartitionSpec as P

slot_block = 16
unroll = 4
core_bit = 1
side_bit = 2
ring_step = 4


def from_everyone(value, axis):
    copies = jnp.broadcast_to(value, (lax.axis_size(axis), *value.shape))
    return lax.all_to_all(copies, axis, split_axis=0, concat_axis=0, tiled=True)


def partner(value, bit):
    return lax.ppermute(value, "ia", [(i, i ^ bit) for i in range(lax.axis_size("ia"))])


def ahead(index, distance):
    ring = lax.axis_size("ia") // ring_step
    return (index // ring_step + distance) % ring * ring_step + index % ring_step


def from_ahead(value, distance):
    size = lax.axis_size("ia")
    return lax.ppermute(value, "ia", [(ahead(i, distance), i) for i in range(size)])


def send_ahead(value, distance):
    size = lax.axis_size("ia")
    return lax.ppermute(value, "ia", [(i, ahead(i, distance)) for i in range(size)])


def relative_rows(row_ids):
    ring = lax.axis_size("ia") // ring_step
    here = lax.axis_index("ia").astype(jnp.int32)
    core = (row_ids ^ here) & 1
    side = ((row_ids ^ here) >> 1) & 1
    along = ((row_ids >> 2) - (here >> 2)) & (ring - 1)
    return core * (2 * ring) + along * 2 + side


def summed(pieces):
    return pieces.astype(jnp.float32).sum(axis=0)


def dense_kernel(rows, cols, norms, count, tiles, near, far, total):
    step = pl.program_id(0)
    edge = tiles.shape[1]
    half_tiles = near.shape[0] // edge
    item_tiles = near.shape[1] // edge

    @pl.when(step == 0)
    def clear():
        def clear_one(index, carry):
            total[index] = jnp.zeros((edge, edge), jnp.float32)
            return carry

        lax.fori_loop(0, total.shape[0], clear_one, 0)

    first = step * slot_block
    live = jnp.clip(count[0] - first, 0, slot_block)

    def add_group(group, carry):
        for lane in range(unroll):
            local = group * unroll + lane
            slot = first + local
            place = rows[slot] * item_tiles + cols[slot]
            norm = jnp.full((8, edge), norms[slot], jnp.int32).astype(jnp.float32)
            scale = jnp.where(slot < count[0], 1.0 / norm, 0.0)
            term = tiles[local].astype(jnp.float32).reshape(edge // 8, 8, edge) * scale[None]
            total[place] = total[place] + term.reshape(edge, edge)
        return carry

    lax.fori_loop(0, (live + unroll - 1) // unroll, add_group, 0)

    @pl.when(step == pl.num_programs(0) - 1)
    def finish():
        def finish_row(row, carry):
            start = pl.multiple_of(row * edge, edge)
            for half, dense in enumerate((near, far)):
                for col in range(item_tiles):
                    place = (half * half_tiles + row) * item_tiles + col
                    dense[pl.ds(start, edge), col * edge : (col + 1) * edge] = total[
                        place
                    ].astype(jnp.bfloat16)
            return carry

        lax.fori_loop(0, half_tiles, finish_row, 0)


def dense_block(tile_block, row_ids, col_ids, norm_ids, count, user_rows, item_rows):
    slots, edge, _ = tile_block.shape
    positions = (user_rows // edge) * (item_rows // edge)
    return pl.pallas_call(
        dense_kernel,
        out_shape=[jax.ShapeDtypeStruct((user_rows // 2, item_rows), jnp.bfloat16)] * 2,
        grid_spec=pltpu.PrefetchScalarGridSpec(
            num_scalar_prefetch=4,
            grid=(slots // slot_block,),
            in_specs=[pl.BlockSpec((slot_block, edge, edge), lambda i, *_: (i, 0, 0))],
            out_specs=[pl.BlockSpec((user_rows // 2, item_rows), lambda i, *_: (0, 0))] * 2,
            scratch_shapes=[pltpu.VMEM((positions, edge, edge), jnp.float32)],
        ),
        compiler_params=pltpu.CompilerParams(
            dimension_semantics=("arbitrary",), vmem_limit_bytes=24 << 20
        ),
        cost_estimate=pl.CostEstimate(
            flops=4 * slots * edge * edge,
            bytes_accessed=2 * slots * edge * edge + 2 * user_rows * item_rows,
            transcendentals=0,
        ),
        name="dense_block",
    )(
        row_ids,
        col_ids,
        norm_ids,
        count,
        pltpu.with_memory_space_constraint(tile_block, pltpu.HBM),
    )


def lay_out_kernel(grad_user, user_emb, grad_item, item_emb, mine, pieces):
    rows = grad_user.shape[0]
    mine[:rows] = grad_user[...]
    mine[rows:] = user_emb[...]
    for peer in range(pieces.shape[0]):
        pieces[peer, 0] = grad_item[...]
        pieces[peer, 1] = item_emb[...]


def lay_out(grad_user, user_emb, grad_item, item_emb):
    peers = lax.axis_size("au")
    return pl.pallas_call(
        lay_out_kernel,
        out_shape=[
            jax.ShapeDtypeStruct((2 * grad_user.shape[0], grad_user.shape[1]), grad_user.dtype),
            jax.ShapeDtypeStruct((peers, 2, *grad_item.shape), grad_item.dtype),
        ],
        name="lay_out",
    )(grad_user, user_emb, grad_item, item_emb)


def product(spec, left, right):
    return jnp.einsum(spec, left, right, preferred_element_type=jnp.float32)


def wide(value):
    return value.astype(jnp.float32)


def device_step(
    user_emb,
    item_emb,
    weight,
    grad_user,
    grad_item,
    tile_values,
    tile_rows,
    tile_cols,
    tile_norm,
    tile_count,
):
    width = weight.shape[0]
    user_rows = user_emb.shape[1] * lax.axis_size("ia")
    item_rows = item_emb.shape[1] * lax.axis_size("au")
    low = jnp.bfloat16
    ring = lax.axis_size("ia") // ring_step

    mine, item_sent = lay_out(grad_user[0], user_emb[0], grad_item[0], item_emb[0])
    beside = partner(mine, side_bit)
    pair = jnp.concatenate([mine, beside])
    own_rows = user_emb.shape[1]
    item_pieces = lax.all_to_all(item_sent, "au", split_axis=0, concat_axis=0, tiled=True)
    parts = [pair]
    for distance in range(1, ring):
        parts.append(from_ahead(pair, distance))
    quarters = [part[i * own_rows : (i + 1) * own_rows] for part in parts for i in range(4)]
    near = jnp.concatenate(quarters[0::2])
    near_emb = jnp.concatenate(quarters[1::2])
    far = partner(near, core_bit)

    items = item_pieces[:, 0].reshape(item_rows, width)
    item_table = item_pieces[:, 1].reshape(item_rows, width)

    dense_near, dense_far = dense_block(
        tile_values[0],
        relative_rows(tile_rows[0]),
        tile_cols[0],
        tile_norm[0],
        tile_count[0],
        user_rows,
        item_rows,
    )
    user_far = product("ui,id->ud", dense_far, items).astype(low)
    user_near = product("ui,id->ud", dense_near, items).astype(low)
    user_sum = wide(user_near) + wide(partner(user_far, core_bit))
    user_sent = user_sum.astype(low)

    item_part = product("ui,ud->id", dense_near, near) + product("ui,ud->id", dense_far, far)
    item_part = item_part.astype(low)
    weight_part = product("rd,re->de", near_emb, user_sent) + product(
        "rd,re->de", item_table, item_part
    )

    peers = lax.axis_size("au")
    pieces = jnp.concatenate(
        [
            item_part.reshape(peers, item_rows // peers, width),
            weight_part.astype(low).reshape(peers, width // peers, width),
        ],
        axis=1,
    )
    arrived = summed(lax.all_to_all(pieces, "au", split_axis=0, concat_axis=0, tiled=True))
    q_item = arrived[: item_rows // peers]
    strip = summed(from_everyone(arrived[item_rows // peers :].astype(low), "ia"))
    user_count = user_rows * lax.axis_size("au")
    item_count = item_rows * lax.axis_size("ia")
    strip = strip / math.sqrt(user_count + item_count)
    grad_weight = wide(from_everyone(strip.astype(low), "au")).reshape(width, width)

    along = user_sum.reshape(ring, user_rows // (2 * ring), width)
    sent = user_sent.reshape(along.shape)
    both = along[0] + sum(wide(send_ahead(sent[d], d)) for d in range(1, ring))
    q_user = both[:own_rows] + wide(partner(both[own_rows:].astype(low), side_bit))

    grad_user_emb = product("re,de->rd", q_user.astype(low), weight).astype(low)
    grad_item_emb = product("re,de->rd", q_item.astype(low), weight).astype(low)
    return (grad_user_emb[None], grad_item_emb[None], grad_weight)


def solution(mesh):
    return jax.shard_map(
        device_step,
        mesh=mesh,
        in_specs=(
            P("au", "ia", None),
            P("ia", "au", None),
            P(),
            P("au", "ia", None),
            P("ia", "au", None),
            P("au", "ia", None, None),
            P("au", "ia"),
            P("au", "ia"),
            P("au", "ia"),
            P("au", "ia"),
        ),
        out_specs=(P("au", "ia", None), P("ia", "au", None), P()),
        check_vma=False,
    )
```

```python
import math

import jax
import jax.numpy as jnp
from jax import lax
from jax.experimental import pallas as pl
from jax.experimental.pallas import tpu as pltpu
from jax.sharding import PartitionSpec as P

slot_block = 16
unroll = 4
core_bit = 1
side_bit = 2
ring_step = 4


def from_everyone(value, axis):
    copies = jnp.broadcast_to(value, (lax.axis_size(axis), *value.shape))
    return lax.all_to_all(copies, axis, split_axis=0, concat_axis=0, tiled=True)


def partner(value, bit):
    return lax.ppermute(value, "ia", [(i, i ^ bit) for i in range(lax.axis_size("ia"))])


def ahead(index, distance):
    ring = lax.axis_size("ia") // ring_step
    return (index // ring_step + distance) % ring * ring_step + index % ring_step


def from_ahead(value, distance):
    size = lax.axis_size("ia")
    return lax.ppermute(value, "ia", [(ahead(i, distance), i) for i in range(size)])


def send_ahead(value, distance):
    size = lax.axis_size("ia")
    return lax.ppermute(value, "ia", [(i, ahead(i, distance)) for i in range(size)])


def relative_rows(row_ids):
    ring = lax.axis_size("ia") // ring_step
    here = lax.axis_index("ia").astype(jnp.int32)
    core = (row_ids ^ here) & 1
    side = ((row_ids ^ here) >> 1) & 1
    along = ((row_ids >> 2) - (here >> 2)) & (ring - 1)
    return core * (2 * ring) + along * 2 + side


def summed(pieces):
    return pieces.astype(jnp.float32).sum(axis=0)


def in_main(value):
    return pltpu.with_memory_space_constraint(value, pltpu.HBM)


def dense_kernel(
    rows, cols, norms, count, tiles_in, near, far, tiles, total, low, in_sems, out_sems
):
    edge = tiles.shape[1]
    item_tiles = near.shape[1] // edge
    half_tiles = near.shape[0] // edge
    chunks = (count[0] + slot_block - 1) // slot_block

    def chunk_copy(chunk):
        slots = pl.ds(chunk * slot_block, slot_block)
        return pltpu.make_async_copy(tiles_in.at[slots], tiles.at[slots], in_sems.at[chunk])

    def fetch(chunk, carry):
        chunk_copy(chunk).start()
        return carry

    lax.fori_loop(0, chunks, fetch, 0)

    def clear(index, carry):
        total[pl.ds(index * 4, 4)] = jnp.zeros((4, edge, edge), jnp.float32)
        return carry

    lax.fori_loop(0, total.shape[0] // 4, clear, 0)

    def add_chunk(chunk, carry):
        chunk_copy(chunk).wait()

        def add_group(group, inner):
            for lane in range(unroll):
                slot = chunk * slot_block + group * unroll + lane
                place = rows[slot] * item_tiles + cols[slot]
                norm = jnp.full((8, edge), norms[slot], jnp.int32).astype(jnp.float32)
                scale = jnp.where(slot < count[0], 1.0 / norm, 0.0)
                term = tiles[slot].astype(jnp.float32).reshape(edge // 8, 8, edge) * scale[None]
                total[place] = total[place] + term.reshape(edge, edge)
            return inner

        return lax.fori_loop(0, slot_block // unroll, add_group, carry)

    lax.fori_loop(0, chunks, add_chunk, 0)

    def row_copy(half, row):
        kept = pl.ds(pl.multiple_of((half * half_tiles + row) * edge, edge), edge)
        out = pl.ds(pl.multiple_of(row * edge, edge), edge)
        dense = near if half == 0 else far
        return pltpu.make_async_copy(
            low.at[kept], dense.at[out], out_sems.at[half * half_tiles + row]
        )

    for half in range(2):

        def finish_row(row, carry):
            start = pl.multiple_of((half * half_tiles + row) * edge, edge)
            for col in range(item_tiles):
                low[pl.ds(start, edge), col * edge : (col + 1) * edge] = total[
                    (half * half_tiles + row) * item_tiles + col
                ].astype(jnp.bfloat16)

            @pl.when(row > 0)
            def send():
                row_copy(half, row - 1).start()

            return carry

        lax.fori_loop(0, half_tiles, finish_row, 0)
        if half == 1:
            row_copy(0, half_tiles - 1).start()
    row_copy(1, half_tiles - 1).start()
    for half in range(2):

        def wait_row(row, carry):
            row_copy(half, row).wait()
            return carry

        lax.fori_loop(0, half_tiles, wait_row, 0)


def dense_block(tile_block, row_ids, col_ids, norm_ids, count, user_rows, item_rows):
    slots, edge, _ = tile_block.shape
    user_tiles = user_rows // edge
    positions = user_tiles * (item_rows // edge)
    in_place = pl.BlockSpec(memory_space=pltpu.HBM)
    return pl.pallas_call(
        dense_kernel,
        out_shape=[pltpu.HBM((user_rows // 2, item_rows), jnp.bfloat16)] * 2,
        grid_spec=pltpu.PrefetchScalarGridSpec(
            num_scalar_prefetch=4,
            grid=(),
            in_specs=[in_place],
            out_specs=[in_place] * 2,
            scratch_shapes=[
                pltpu.VMEM((slots, edge, edge), jnp.bfloat16),
                pltpu.VMEM((positions, edge, edge), jnp.float32),
                pltpu.VMEM((user_rows, item_rows), jnp.bfloat16),
                pltpu.SemaphoreType.DMA((slots // slot_block,)),
                pltpu.SemaphoreType.DMA((user_tiles,)),
            ],
        ),
        compiler_params=pltpu.CompilerParams(vmem_limit_bytes=24 << 20),
        cost_estimate=pl.CostEstimate(
            flops=4 * slots * edge * edge,
            bytes_accessed=2 * slots * edge * edge + 2 * user_rows * item_rows,
            transcendentals=0,
        ),
        name="dense_block",
    )(row_ids, col_ids, norm_ids, count, in_main(tile_block))


def join_kernel(mine, beside, pair):
    rows = mine.shape[0]
    pair[:rows] = mine[...]
    pair[rows:] = beside[...]


def join(mine, beside):
    rows, width = mine.shape
    return pl.pallas_call(
        join_kernel, out_shape=jax.ShapeDtypeStruct((2 * rows, width), mine.dtype), name="join"
    )(in_main(mine), in_main(beside))


def assemble_kernel(*refs):
    *parts, near, near_emb = refs
    rows = parts[0].shape[0] // 4
    for index, part in enumerate(parts):
        for side in range(2):
            out = pl.ds((2 * index + side) * rows, rows)
            near[out] = part[pl.ds(2 * side * rows, rows)]
            near_emb[out] = part[pl.ds((2 * side + 1) * rows, rows)]


def assemble(parts):
    rows, width = parts[0].shape
    shape = jax.ShapeDtypeStruct((len(parts) * rows // 2, width), parts[0].dtype)
    return pl.pallas_call(assemble_kernel, out_shape=[shape] * 2, name="assemble")(*map(in_main, parts))


def lay_out_kernel(grad_user, user_emb, grad_item, item_emb, mine, pieces):
    rows = grad_user.shape[0]
    mine[:rows] = grad_user[...]
    mine[rows:] = user_emb[...]
    for peer in range(pieces.shape[0]):
        pieces[peer, 0] = grad_item[...]
        pieces[peer, 1] = item_emb[...]


def lay_out(grad_user, user_emb, grad_item, item_emb):
    peers = lax.axis_size("au")
    return pl.pallas_call(
        lay_out_kernel,
        out_shape=[
            jax.ShapeDtypeStruct((2 * grad_user.shape[0], grad_user.shape[1]), grad_user.dtype),
            jax.ShapeDtypeStruct((peers, 2, *grad_item.shape), grad_item.dtype),
        ],
        name="lay_out",
    )(grad_user, user_emb, grad_item, item_emb)


def product(spec, left, right):
    return jnp.einsum(spec, left, right, preferred_element_type=jnp.float32)


def wide(value):
    return value.astype(jnp.float32)


def device_step(
    user_emb,
    item_emb,
    weight,
    grad_user,
    grad_item,
    tile_values,
    tile_rows,
    tile_cols,
    tile_norm,
    tile_count,
):
    width = weight.shape[0]
    user_rows = user_emb.shape[1] * lax.axis_size("ia")
    item_rows = item_emb.shape[1] * lax.axis_size("au")
    low = jnp.bfloat16
    ring = lax.axis_size("ia") // ring_step

    mine, item_sent = lay_out(grad_user[0], user_emb[0], grad_item[0], item_emb[0])
    beside = partner(mine, side_bit)
    pair = join(mine, beside)
    own_rows = user_emb.shape[1]
    item_pieces = lax.all_to_all(item_sent, "au", split_axis=0, concat_axis=0, tiled=True)
    parts = [pair]
    for distance in range(1, ring):
        parts.append(from_ahead(pair, distance))
    near, near_emb = assemble(parts)
    far = partner(near, core_bit)

    items = item_pieces[:, 0].reshape(item_rows, width)
    item_table = item_pieces[:, 1].reshape(item_rows, width)

    dense_near, dense_far = dense_block(
        tile_values[0],
        relative_rows(tile_rows[0]),
        tile_cols[0],
        tile_norm[0],
        tile_count[0],
        user_rows,
        item_rows,
    )
    user_far = product("ui,id->ud", dense_far, items).astype(low)
    user_near = product("ui,id->ud", dense_near, items).astype(low)
    user_sum = wide(user_near) + wide(partner(user_far, core_bit))
    user_sent = user_sum.astype(low)

    item_part = product("ui,ud->id", dense_near, near) + product("ui,ud->id", dense_far, far)
    item_part = item_part.astype(low)
    weight_part = product("rd,re->de", near_emb, user_sent) + product(
        "rd,re->de", item_table, item_part
    )

    peers = lax.axis_size("au")
    pieces = jnp.concatenate(
        [
            item_part.reshape(peers, item_rows // peers, width),
            weight_part.astype(low).reshape(peers, width // peers, width),
        ],
        axis=1,
    )
    arrived = summed(lax.all_to_all(pieces, "au", split_axis=0, concat_axis=0, tiled=True))
    q_item = arrived[: item_rows // peers]
    strip = summed(from_everyone(arrived[item_rows // peers :].astype(low), "ia"))
    user_count = user_rows * lax.axis_size("au")
    item_count = item_rows * lax.axis_size("ia")
    strip = strip / math.sqrt(user_count + item_count)
    grad_weight = wide(from_everyone(strip.astype(low), "au")).reshape(width, width)

    along = user_sum.reshape(ring, user_rows // (2 * ring), width)
    sent = user_sent.reshape(along.shape)
    both = along[0] + sum(wide(send_ahead(sent[d], d)) for d in range(1, ring))
    q_user = both[:own_rows] + wide(partner(both[own_rows:].astype(low), side_bit))

    grad_user_emb = product("re,de->rd", q_user.astype(low), weight).astype(low)
    grad_item_emb = product("re,de->rd", q_item.astype(low), weight).astype(low)
    return (grad_user_emb[None], grad_item_emb[None], grad_weight)


def solution(mesh):
    return jax.shard_map(
        device_step,
        mesh=mesh,
        in_specs=(
            P("au", "ia", None),
            P("ia", "au", None),
            P(),
            P("au", "ia", None),
            P("ia", "au", None),
            P("au", "ia", None, None),
            P("au", "ia"),
            P("au", "ia"),
            P("au", "ia"),
            P("au", "ia"),
        ),
        out_specs=(P("au", "ia", None), P("ia", "au", None), P()),
        check_vma=False,
    )
```

```python
import math

import jax
import jax.numpy as jnp
from jax import lax
from jax.experimental import pallas as pl
from jax.experimental.pallas import tpu as pltpu
from jax.sharding import PartitionSpec as P

slot_block = 16
unroll = 4
core_bit = 1
side_bit = 2
ring_step = 4


def from_everyone(value, axis):
    copies = jnp.broadcast_to(value, (lax.axis_size(axis), *value.shape))
    return lax.all_to_all(copies, axis, split_axis=0, concat_axis=0, tiled=True)


def partner(value, bit):
    return lax.ppermute(value, "ia", [(i, i ^ bit) for i in range(lax.axis_size("ia"))])


def ahead(index, distance):
    ring = lax.axis_size("ia") // ring_step
    return (index // ring_step + distance) % ring * ring_step + index % ring_step


def from_ahead(value, distance):
    size = lax.axis_size("ia")
    return lax.ppermute(value, "ia", [(ahead(i, distance), i) for i in range(size)])


def send_ahead(value, distance):
    size = lax.axis_size("ia")
    return lax.ppermute(value, "ia", [(i, ahead(i, distance)) for i in range(size)])


def relative_rows(row_ids):
    ring = lax.axis_size("ia") // ring_step
    here = lax.axis_index("ia").astype(jnp.int32)
    core = (row_ids ^ here) & 1
    side = ((row_ids ^ here) >> 1) & 1
    along = ((row_ids >> 2) - (here >> 2)) & (ring - 1)
    return core * (2 * ring) + along * 2 + side


def summed(pieces):
    return pieces.astype(jnp.float32).sum(axis=0)


def in_main(value):
    return pltpu.with_memory_space_constraint(value, pltpu.HBM)


def dense_kernel(
    rows, cols, norms, count, tiles_in, near, far, tiles, total, low, in_sems, out_sems
):
    edge = tiles.shape[1]
    item_tiles = near.shape[1] // edge
    half_tiles = near.shape[0] // edge
    chunks = (count[0] + slot_block - 1) // slot_block

    def chunk_copy(chunk):
        slots = pl.ds(chunk * slot_block, slot_block)
        return pltpu.make_async_copy(tiles_in.at[slots], tiles.at[slots], in_sems.at[chunk])

    def fetch(chunk, carry):
        chunk_copy(chunk).start()
        return carry

    lax.fori_loop(0, chunks, fetch, 0)

    def clear(index, carry):
        total[pl.ds(index * 4, 4)] = jnp.zeros((4, edge, edge), jnp.float32)
        return carry

    lax.fori_loop(0, total.shape[0] // 4, clear, 0)

    def add_chunk(chunk, carry):
        chunk_copy(chunk).wait()

        def add_group(group, inner):
            for lane in range(unroll):
                slot = chunk * slot_block + group * unroll + lane
                place = rows[slot] * item_tiles + cols[slot]
                norm = jnp.full((8, edge), norms[slot], jnp.int32).astype(jnp.float32)
                scale = jnp.where(slot < count[0], 1.0 / norm, 0.0)
                term = tiles[slot].astype(jnp.float32).reshape(edge // 8, 8, edge) * scale[None]
                total[place] = total[place] + term.reshape(edge, edge)
            return inner

        return lax.fori_loop(0, slot_block // unroll, add_group, carry)

    lax.fori_loop(0, chunks, add_chunk, 0)

    def row_copy(half, row):
        kept = pl.ds(pl.multiple_of((half * half_tiles + row) * edge, edge), edge)
        out = pl.ds(pl.multiple_of(row * edge, edge), edge)
        dense = near if half == 0 else far
        return pltpu.make_async_copy(
            low.at[kept], dense.at[out], out_sems.at[half * half_tiles + row]
        )

    for half in range(2):

        def finish_row(row, carry):
            start = pl.multiple_of((half * half_tiles + row) * edge, edge)
            for col in range(item_tiles):
                low[pl.ds(start, edge), col * edge : (col + 1) * edge] = total[
                    (half * half_tiles + row) * item_tiles + col
                ].astype(jnp.bfloat16)

            @pl.when(row > 0)
            def send():
                row_copy(half, row - 1).start()

            return carry

        lax.fori_loop(0, half_tiles, finish_row, 0)
        if half == 1:
            row_copy(0, half_tiles - 1).start()
    row_copy(1, half_tiles - 1).start()
    for half in range(2):

        def wait_row(row, carry):
            row_copy(half, row).wait()
            return carry

        lax.fori_loop(0, half_tiles, wait_row, 0)


def dense_block(tile_block, row_ids, col_ids, norm_ids, count, user_rows, item_rows):
    slots, edge, _ = tile_block.shape
    user_tiles = user_rows // edge
    positions = user_tiles * (item_rows // edge)
    in_place = pl.BlockSpec(memory_space=pltpu.HBM)
    return pl.pallas_call(
        dense_kernel,
        out_shape=[pltpu.HBM((user_rows // 2, item_rows), jnp.bfloat16)] * 2,
        grid_spec=pltpu.PrefetchScalarGridSpec(
            num_scalar_prefetch=4,
            grid=(),
            in_specs=[in_place],
            out_specs=[in_place] * 2,
            scratch_shapes=[
                pltpu.VMEM((slots, edge, edge), jnp.bfloat16),
                pltpu.VMEM((positions, edge, edge), jnp.float32),
                pltpu.VMEM((user_rows, item_rows), jnp.bfloat16),
                pltpu.SemaphoreType.DMA((slots // slot_block,)),
                pltpu.SemaphoreType.DMA((user_tiles,)),
            ],
        ),
        compiler_params=pltpu.CompilerParams(vmem_limit_bytes=24 << 20),
        cost_estimate=pl.CostEstimate(
            flops=4 * slots * edge * edge,
            bytes_accessed=2 * slots * edge * edge + 2 * user_rows * item_rows,
            transcendentals=0,
        ),
        name="dense_block",
    )(row_ids, col_ids, norm_ids, count, in_main(tile_block))


def join_kernel(mine, beside, pair):
    rows = mine.shape[0]
    pair[:rows] = mine[...]
    pair[rows:] = beside[...]


def join(mine, beside):
    rows, width = mine.shape
    return pl.pallas_call(
        join_kernel, out_shape=jax.ShapeDtypeStruct((2 * rows, width), mine.dtype), name="join"
    )(in_main(mine), in_main(beside))


def assemble_kernel(*refs):
    *parts, near, near_emb = refs
    rows = parts[0].shape[0] // 4
    for index, part in enumerate(parts):
        for side in range(2):
            out = pl.ds((2 * index + side) * rows, rows)
            near[out] = part[pl.ds(2 * side * rows, rows)]
            near_emb[out] = part[pl.ds((2 * side + 1) * rows, rows)]


def assemble(parts):
    rows, width = parts[0].shape
    shape = jax.ShapeDtypeStruct((len(parts) * rows // 2, width), parts[0].dtype)
    return pl.pallas_call(assemble_kernel, out_shape=[shape] * 2, name="assemble")(*map(in_main, parts))


def lay_out_kernel(grad_user, user_emb, grad_item, item_emb, mine, pieces):
    rows = grad_user.shape[0]
    mine[:rows] = grad_user[...]
    mine[rows:] = user_emb[...]
    for peer in range(pieces.shape[0]):
        pieces[peer, 0] = grad_item[...]
        pieces[peer, 1] = item_emb[...]


def lay_out(grad_user, user_emb, grad_item, item_emb):
    peers = lax.axis_size("au")
    return pl.pallas_call(
        lay_out_kernel,
        out_shape=[
            jax.ShapeDtypeStruct((2 * grad_user.shape[0], grad_user.shape[1]), grad_user.dtype),
            jax.ShapeDtypeStruct((peers, 2, *grad_item.shape), grad_item.dtype),
        ],
        name="lay_out",
    )(grad_user, user_emb, grad_item, item_emb)


def product(spec, left, right):
    return jnp.einsum(spec, left, right, preferred_element_type=jnp.float32)


def wide(value):
    return value.astype(jnp.float32)


def device_step(
    user_emb,
    item_emb,
    weight,
    grad_user,
    grad_item,
    tile_values,
    tile_rows,
    tile_cols,
    tile_norm,
    tile_count,
):
    width = weight.shape[0]
    user_rows = user_emb.shape[1] * lax.axis_size("ia")
    item_rows = item_emb.shape[1] * lax.axis_size("au")
    low = jnp.bfloat16
    ring = lax.axis_size("ia") // ring_step

    mine, item_sent = lay_out(grad_user[0], user_emb[0], grad_item[0], item_emb[0])
    beside = partner(mine, side_bit)
    pair = join(mine, beside)
    own_rows = user_emb.shape[1]
    item_pieces = lax.all_to_all(item_sent, "au", split_axis=0, concat_axis=0, tiled=True)
    parts = [pair]
    for distance in range(1, ring):
        parts.append(from_ahead(pair, distance))
    near, near_emb = assemble(parts)
    far = partner(near, core_bit)
    far_emb = partner(near_emb, core_bit)

    items = item_pieces[:, 0].reshape(item_rows, width)
    item_table = item_pieces[:, 1].reshape(item_rows, width)

    dense_near, dense_far = dense_block(
        tile_values[0],
        relative_rows(tile_rows[0]),
        tile_cols[0],
        tile_norm[0],
        tile_count[0],
        user_rows,
        item_rows,
    )
    user_far = product("ui,id->ud", dense_far, items).astype(low)
    user_near = product("ui,id->ud", dense_near, items).astype(low)
    user_far, user_near = lax.optimization_barrier((user_far, user_near))
    item_part = product("ui,ud->id", dense_near, near) + product("ui,ud->id", dense_far, far)
    item_part = item_part.astype(low)
    weight_part = (
        product("rd,re->de", near_emb, user_near)
        + product("rd,re->de", far_emb, user_far)
        + product("rd,re->de", item_table, item_part)
    )

    peers = lax.axis_size("au")
    pieces = jnp.concatenate(
        [
            item_part.reshape(peers, item_rows // peers, width),
            weight_part.astype(low).reshape(peers, width // peers, width),
        ],
        axis=1,
    )
    arrived = lax.all_to_all(pieces, "au", split_axis=0, concat_axis=0, tiled=True)
    arrived = summed(arrived)
    q_item = arrived[: item_rows // peers]
    strip = summed(from_everyone(arrived[item_rows // peers :].astype(low), "ia"))
    user_count = user_rows * lax.axis_size("au")
    item_count = item_rows * lax.axis_size("ia")
    strip = strip / math.sqrt(user_count + item_count)
    grad_weight = wide(from_everyone(strip.astype(low), "au")).reshape(width, width)

    across = partner(user_far, core_bit)
    along = (wide(user_near) + wide(across)).reshape(ring, user_rows // (2 * ring), width)
    sent = along.astype(low)
    both = along[0] + sum(wide(send_ahead(sent[d], d)) for d in range(1, ring))
    q_user = both[:own_rows] + wide(partner(both[own_rows:].astype(low), side_bit))

    grad_user_emb = product("re,de->rd", q_user.astype(low), weight).astype(low)
    grad_item_emb = product("re,de->rd", q_item.astype(low), weight).astype(low)
    return (grad_user_emb[None], grad_item_emb[None], grad_weight)


def solution(mesh):
    return jax.shard_map(
        device_step,
        mesh=mesh,
        in_specs=(
            P("au", "ia", None),
            P("ia", "au", None),
            P(),
            P("au", "ia", None),
            P("ia", "au", None),
            P("au", "ia", None, None),
            P("au", "ia"),
            P("au", "ia"),
            P("au", "ia"),
            P("au", "ia"),
        ),
        out_specs=(P("au", "ia", None), P("ia", "au", None), P()),
        check_vma=False,
    )
```

```python
import math

import jax
import jax.numpy as jnp
from jax import lax
from jax.experimental import pallas as pl
from jax.experimental.pallas import tpu as pltpu
from jax.sharding import PartitionSpec as P

slot_block = 16
unroll = 4
core_bit = 1
side_bit = 2
ring_step = 4


def from_everyone(value, axis):
    copies = jnp.broadcast_to(value, (lax.axis_size(axis), *value.shape))
    return lax.all_to_all(copies, axis, split_axis=0, concat_axis=0, tiled=True)


def partner(value, bit):
    return lax.ppermute(value, "ia", [(i, i ^ bit) for i in range(lax.axis_size("ia"))])


def ahead(index, distance):
    ring = lax.axis_size("ia") // ring_step
    return (index // ring_step + distance) % ring * ring_step + index % ring_step


def from_ahead(value, distance):
    size = lax.axis_size("ia")
    return lax.ppermute(value, "ia", [(ahead(i, distance), i) for i in range(size)])


def send_ahead(value, distance):
    size = lax.axis_size("ia")
    return lax.ppermute(value, "ia", [(i, ahead(i, distance)) for i in range(size)])


def relative_rows(row_ids):
    ring = lax.axis_size("ia") // ring_step
    here = lax.axis_index("ia").astype(jnp.int32)
    core = (row_ids ^ here) & 1
    side = ((row_ids ^ here) >> 1) & 1
    along = ((row_ids >> 2) - (here >> 2)) & (ring - 1)
    return core * (2 * ring) + along * 2 + side


def summed(pieces):
    return pieces.astype(jnp.float32).sum(axis=0)


def in_main(value):
    return pltpu.with_memory_space_constraint(value, pltpu.HBM)


def dense_kernel(
    rows, cols, norms, count, tiles_in, near, far, tiles, total, low, in_sems, out_sems
):
    edge = tiles.shape[1]
    item_tiles = near.shape[1] // edge
    half_tiles = near.shape[0] // edge
    chunks = (count[0] + slot_block - 1) // slot_block

    def chunk_copy(chunk):
        slots = pl.ds(chunk * slot_block, slot_block)
        return pltpu.make_async_copy(tiles_in.at[slots], tiles.at[slots], in_sems.at[chunk])

    def fetch(chunk, carry):
        chunk_copy(chunk).start()
        return carry

    lax.fori_loop(0, chunks, fetch, 0)

    def clear(index, carry):
        total[pl.ds(index * 4, 4)] = jnp.zeros((4, edge, edge), jnp.float32)
        return carry

    lax.fori_loop(0, total.shape[0] // 4, clear, 0)

    def add_chunk(chunk, carry):
        chunk_copy(chunk).wait()

        def add_group(group, inner):
            for lane in range(unroll):
                slot = chunk * slot_block + group * unroll + lane
                place = rows[slot] * item_tiles + cols[slot]
                norm = jnp.full((8, edge), norms[slot], jnp.int32).astype(jnp.float32)
                scale = jnp.where(slot < count[0], 1.0 / norm, 0.0)
                term = tiles[slot].astype(jnp.float32).reshape(edge // 8, 8, edge) * scale[None]
                total[place] = total[place] + term.reshape(edge, edge)
            return inner

        return lax.fori_loop(0, slot_block // unroll, add_group, carry)

    lax.fori_loop(0, chunks, add_chunk, 0)

    def row_copy(half, row):
        kept = pl.ds(pl.multiple_of((half * half_tiles + row) * edge, edge), edge)
        out = pl.ds(pl.multiple_of(row * edge, edge), edge)
        dense = near if half == 0 else far
        return pltpu.make_async_copy(
            low.at[kept], dense.at[out], out_sems.at[half * half_tiles + row]
        )

    for half in range(2):

        def finish_row(row, carry):
            start = pl.multiple_of((half * half_tiles + row) * edge, edge)
            for col in range(item_tiles):
                low[pl.ds(start, edge), col * edge : (col + 1) * edge] = total[
                    (half * half_tiles + row) * item_tiles + col
                ].astype(jnp.bfloat16)

            @pl.when(row > 0)
            def send():
                row_copy(half, row - 1).start()

            return carry

        lax.fori_loop(0, half_tiles, finish_row, 0)
        if half == 1:
            row_copy(0, half_tiles - 1).start()
    row_copy(1, half_tiles - 1).start()
    for half in range(2):

        def wait_row(row, carry):
            row_copy(half, row).wait()
            return carry

        lax.fori_loop(0, half_tiles, wait_row, 0)


def dense_block(tile_block, row_ids, col_ids, norm_ids, count, user_rows, item_rows):
    slots, edge, _ = tile_block.shape
    user_tiles = user_rows // edge
    positions = user_tiles * (item_rows // edge)
    in_place = pl.BlockSpec(memory_space=pltpu.HBM)
    return pl.pallas_call(
        dense_kernel,
        out_shape=[pltpu.HBM((user_rows // 2, item_rows), jnp.bfloat16)] * 2,
        grid_spec=pltpu.PrefetchScalarGridSpec(
            num_scalar_prefetch=4,
            grid=(),
            in_specs=[in_place],
            out_specs=[in_place] * 2,
            scratch_shapes=[
                pltpu.VMEM((slots, edge, edge), jnp.bfloat16),
                pltpu.VMEM((positions, edge, edge), jnp.float32),
                pltpu.VMEM((user_rows, item_rows), jnp.bfloat16),
                pltpu.SemaphoreType.DMA((slots // slot_block,)),
                pltpu.SemaphoreType.DMA((user_tiles,)),
            ],
        ),
        compiler_params=pltpu.CompilerParams(vmem_limit_bytes=24 << 20),
        cost_estimate=pl.CostEstimate(
            flops=4 * slots * edge * edge,
            bytes_accessed=2 * slots * edge * edge + 2 * user_rows * item_rows,
            transcendentals=0,
        ),
        name="dense_block",
    )(row_ids, col_ids, norm_ids, count, in_main(tile_block))


def assemble_kernel(*refs):
    *parts, near = refs
    rows = parts[0].shape[0] // 4
    table = near.shape[0] // 2
    for index, part in enumerate(parts):
        for side in range(2):
            place = (2 * index + side) * rows
            near[pl.ds(place, rows)] = part[pl.ds(2 * side * rows, rows)]
            near[pl.ds(table + place, rows)] = part[pl.ds((2 * side + 1) * rows, rows)]


def assemble(parts):
    rows, width = parts[0].shape
    shape = jax.ShapeDtypeStruct((len(parts) * rows, width), parts[0].dtype)
    return pl.pallas_call(assemble_kernel, out_shape=shape, name="assemble")(*map(in_main, parts))


def lay_out_kernel(grad_user, user_emb, grad_item, item_emb, mine, pair, pieces):
    rows = grad_user.shape[0]
    mine[:rows] = grad_user[...]
    mine[rows:] = user_emb[...]
    pair[:rows] = grad_user[...]
    pair[rows : 2 * rows] = user_emb[...]
    pair[2 * rows :] = jnp.zeros((2 * rows, pair.shape[1]), pair.dtype)
    item_rows = grad_item.shape[0]
    for peer in range(pieces.shape[0]):
        pieces[peer, :item_rows] = grad_item[...]
        pieces[peer, item_rows:] = item_emb[...]


def lay_out(grad_user, user_emb, grad_item, item_emb):
    peers = lax.axis_size("au")
    rows, width = grad_user.shape
    return pl.pallas_call(
        lay_out_kernel,
        out_shape=[
            jax.ShapeDtypeStruct((2 * rows, width), grad_user.dtype),
            jax.ShapeDtypeStruct((4 * rows, width), grad_user.dtype),
            jax.ShapeDtypeStruct((peers, 2 * grad_item.shape[0], width), grad_item.dtype),
        ],
        name="lay_out",
    )(grad_user, user_emb, grad_item, item_emb)


def transposed_product(left, right):
    return lax.dot_general(
        left, right, (((0,), (0,)), ((), ())), preferred_element_type=jnp.float32
    )


def finish_kernel(
    dense_near,
    dense_far,
    item_in,
    near_in,
    far_in,
    user_near,
    user_far,
    pieces,
    dense,
    item_rows,
    sources,
    q_turned,
    sems,
):
    low = jnp.bfloat16
    peers, both_rows, width = item_rows.shape
    piece_rows = both_rows // 2
    half_rows, all_items = dense.shape[1:]
    step = 256
    item_copy = pltpu.make_async_copy(item_in, item_rows, sems.at[0])
    dense_copies = [
        pltpu.make_async_copy(ref, dense.at[half], sems.at[1 + half])
        for half, ref in enumerate((dense_near, dense_far))
    ]
    source_copies = [
        pltpu.make_async_copy(ref, sources.at[half], sems.at[3 + half])
        for half, ref in enumerate((near_in, far_in))
    ]
    item_copy.start()
    for half in range(2):
        dense_copies[half].start()
        source_copies[half].start()
    item_copy.wait()
    items = item_rows[:, :piece_rows].reshape(all_items, width)
    weight_term = jnp.zeros((width, width), jnp.float32)
    for half, user in enumerate((user_near, user_far)):
        dense_copies[half].wait()
        for start in range(0, half_rows, step):
            rows = dense[half, start : start + step]
            user[start : start + step] = jnp.dot(
                rows, items, preferred_element_type=jnp.float32
            ).astype(low)
        source_copies[half].wait()
        weight_term += transposed_product(sources[half, half_rows:], user[...])
        turned = sources[half, :half_rows].T
        for start in range(0, all_items, step):
            part = jnp.dot(
                turned, dense[half, :, start : start + step], preferred_element_type=jnp.float32
            )
            if half == 0:
                q_turned[:, start : start + step] = part
            else:
                q_turned[:, start : start + step] += part
    q_low = q_turned[...].astype(low)
    table = item_rows[:, piece_rows:].reshape(all_items, width)
    weight_term += jnp.dot(q_low, table, preferred_element_type=jnp.float32).T
    pieces[:, :piece_rows] = q_turned[...].T.astype(low).reshape(peers, piece_rows, width)
    pieces[:, piece_rows:] = weight_term.reshape(peers, width // peers, width).astype(low)


def finish(dense_near, dense_far, item_pieces, near, far):
    half_rows, all_items = dense_near.shape
    peers, both_rows, width = item_pieces.shape
    low = jnp.bfloat16
    strip = both_rows // 2 + width // peers
    in_place = pl.BlockSpec(memory_space=pltpu.HBM)
    return pl.pallas_call(
        finish_kernel,
        in_specs=[in_place] * 5,
        out_shape=[
            jax.ShapeDtypeStruct((half_rows, width), low),
            jax.ShapeDtypeStruct((half_rows, width), low),
            jax.ShapeDtypeStruct((peers, strip, width), low),
        ],
        scratch_shapes=[
            pltpu.VMEM((2, half_rows, all_items), low),
            pltpu.VMEM((peers, both_rows, width), low),
            pltpu.VMEM((2, 2 * half_rows, width), low),
            pltpu.VMEM((width, all_items), jnp.float32),
            pltpu.SemaphoreType.DMA((5,)),
        ],
        compiler_params=pltpu.CompilerParams(vmem_limit_bytes=32 << 20),
        cost_estimate=pl.CostEstimate(
            flops=8 * half_rows * all_items * width,
            bytes_accessed=4 * half_rows * all_items + 8 * half_rows * width,
            transcendentals=0,
        ),
        name="finish",
    )(*map(in_main, (dense_near, dense_far, item_pieces, near, far)))


def product(spec, left, right):
    return jnp.einsum(spec, left, right, preferred_element_type=jnp.float32)


def wide(value):
    return value.astype(jnp.float32)


def device_step(
    user_emb,
    item_emb,
    weight,
    grad_user,
    grad_item,
    tile_values,
    tile_rows,
    tile_cols,
    tile_norm,
    tile_count,
):
    width = weight.shape[0]
    user_rows = user_emb.shape[1] * lax.axis_size("ia")
    item_rows = item_emb.shape[1] * lax.axis_size("au")
    low = jnp.bfloat16
    ring = lax.axis_size("ia") // ring_step

    mine, pair, item_sent = lay_out(grad_user[0], user_emb[0], grad_item[0], item_emb[0])
    beside = partner(mine, side_bit)
    pair = lax.dynamic_update_slice(pair, beside, (mine.shape[0], 0))
    own_rows = user_emb.shape[1]
    item_pieces = lax.all_to_all(item_sent, "au", split_axis=0, concat_axis=0, tiled=True)
    parts = [pair]
    for distance in range(1, ring):
        parts.append(from_ahead(pair, distance))
    near = assemble(parts)
    far = partner(near, core_bit)

    dense_near, dense_far = dense_block(
        tile_values[0],
        relative_rows(tile_rows[0]),
        tile_cols[0],
        tile_norm[0],
        tile_count[0],
        user_rows,
        item_rows,
    )
    user_near, user_far, pieces = finish(dense_near, dense_far, item_pieces, near, far)
    peers = lax.axis_size("au")
    arrived = lax.all_to_all(pieces, "au", split_axis=0, concat_axis=0, tiled=True)
    arrived = summed(arrived)
    q_item = arrived[: item_rows // peers]
    strip = summed(from_everyone(arrived[item_rows // peers :].astype(low), "ia"))
    user_count = user_rows * lax.axis_size("au")
    item_count = item_rows * lax.axis_size("ia")
    strip = strip / math.sqrt(user_count + item_count)
    grad_weight = wide(from_everyone(strip.astype(low), "au")).reshape(width, width)

    across = partner(user_far, core_bit)
    along = (wide(user_near) + wide(across)).reshape(ring, user_rows // (2 * ring), width)
    sent = along.astype(low)
    both = along[0] + sum(wide(send_ahead(sent[d], d)) for d in range(1, ring))
    q_user = both[:own_rows] + wide(partner(both[own_rows:].astype(low), side_bit))

    grad_user_emb = product("re,de->rd", q_user.astype(low), weight).astype(low)
    grad_item_emb = product("re,de->rd", q_item.astype(low), weight).astype(low)
    return (grad_user_emb[None], grad_item_emb[None], grad_weight)


def solution(mesh):
    return jax.shard_map(
        device_step,
        mesh=mesh,
        in_specs=(
            P("au", "ia", None),
            P("ia", "au", None),
            P(),
            P("au", "ia", None),
            P("ia", "au", None),
            P("au", "ia", None, None),
            P("au", "ia"),
            P("au", "ia"),
            P("au", "ia"),
            P("au", "ia"),
        ),
        out_specs=(P("au", "ia", None), P("ia", "au", None), P()),
        check_vma=False,
    )
```

```python
import math

import jax
import jax.numpy as jnp
from jax import lax
from jax.experimental import pallas as pl
from jax.experimental.pallas import tpu as pltpu
from jax.sharding import PartitionSpec as P

slot_block = 16
unroll = 4
step = 256
core_bit = 1
side_bit = 2
ring_step = 4


def from_everyone(value, axis):
    copies = jnp.broadcast_to(value, (lax.axis_size(axis), *value.shape))
    return lax.all_to_all(copies, axis, split_axis=0, concat_axis=0, tiled=True)


def partner(value, bit):
    return lax.ppermute(value, "ia", [(i, i ^ bit) for i in range(lax.axis_size("ia"))])


def ahead(index, distance):
    ring = lax.axis_size("ia") // ring_step
    return (index // ring_step + distance) % ring * ring_step + index % ring_step


def from_ahead(value, distance):
    size = lax.axis_size("ia")
    return lax.ppermute(value, "ia", [(ahead(i, distance), i) for i in range(size)])


def send_ahead(value, distance):
    size = lax.axis_size("ia")
    return lax.ppermute(value, "ia", [(i, ahead(i, distance)) for i in range(size)])


def relative_rows(row_ids):
    ring = lax.axis_size("ia") // ring_step
    here = lax.axis_index("ia").astype(jnp.int32)
    core = (row_ids ^ here) & 1
    side = ((row_ids ^ here) >> 1) & 1
    along = ((row_ids >> 2) - (here >> 2)) & (ring - 1)
    return core * (2 * ring) + along * 2 + side


def summed(pieces):
    return pieces.astype(jnp.float32).sum(axis=0)


def in_main(value):
    return pltpu.with_memory_space_constraint(value, pltpu.HBM)


def dense_kernel(
    rows, cols, norms, count, tiles_in, near, far, tiles, total, low, in_sems, out_sems
):
    edge = tiles.shape[1]
    item_tiles = near.shape[1] // edge
    half_tiles = near.shape[0] // edge
    chunks = (count[0] + slot_block - 1) // slot_block

    def chunk_copy(chunk):
        slots = pl.ds(chunk * slot_block, slot_block)
        return pltpu.make_async_copy(tiles_in.at[slots], tiles.at[slots], in_sems.at[chunk])

    def fetch(chunk, carry):
        chunk_copy(chunk).start()
        return carry

    lax.fori_loop(0, chunks, fetch, 0)

    def clear(index, carry):
        total[pl.ds(index * 4, 4)] = jnp.zeros((4, edge, edge), jnp.float32)
        return carry

    lax.fori_loop(0, total.shape[0] // 4, clear, 0)

    def add_chunk(chunk, carry):
        chunk_copy(chunk).wait()

        def add_group(group, inner):
            for lane in range(unroll):
                slot = chunk * slot_block + group * unroll + lane
                place = rows[slot] * item_tiles + cols[slot]
                norm = jnp.full((8, edge), norms[slot], jnp.int32).astype(jnp.float32)
                scale = jnp.where(slot < count[0], 1.0 / norm, 0.0)
                term = tiles[slot].astype(jnp.float32).reshape(edge // 8, 8, edge) * scale[None]
                total[place] = total[place] + term.reshape(edge, edge)
            return inner

        return lax.fori_loop(0, slot_block // unroll, add_group, carry)

    lax.fori_loop(0, chunks, add_chunk, 0)

    def row_copy(half, row):
        kept = pl.ds(pl.multiple_of((half * half_tiles + row) * edge, edge), edge)
        out = pl.ds(pl.multiple_of(row * edge, edge), edge)
        dense = near if half == 0 else far
        return pltpu.make_async_copy(
            low.at[kept], dense.at[out], out_sems.at[half * half_tiles + row]
        )

    for half in range(2):

        def finish_row(row, carry):
            start = pl.multiple_of((half * half_tiles + row) * edge, edge)
            for col in range(item_tiles):
                low[pl.ds(start, edge), col * edge : (col + 1) * edge] = total[
                    (half * half_tiles + row) * item_tiles + col
                ].astype(jnp.bfloat16)

            @pl.when(row > 0)
            def send():
                row_copy(half, row - 1).start()

            return carry

        lax.fori_loop(0, half_tiles, finish_row, 0)
        if half == 1:
            row_copy(0, half_tiles - 1).start()
    row_copy(1, half_tiles - 1).start()
    for half in range(2):

        def wait_row(row, carry):
            row_copy(half, row).wait()
            return carry

        lax.fori_loop(0, half_tiles, wait_row, 0)


def dense_block(tile_block, row_ids, col_ids, norm_ids, count, user_rows, item_rows):
    slots, edge, _ = tile_block.shape
    user_tiles = user_rows // edge
    positions = user_tiles * (item_rows // edge)
    in_place = pl.BlockSpec(memory_space=pltpu.HBM)
    return pl.pallas_call(
        dense_kernel,
        out_shape=[pltpu.HBM((user_rows // 2, item_rows), jnp.bfloat16)] * 2,
        grid_spec=pltpu.PrefetchScalarGridSpec(
            num_scalar_prefetch=4,
            grid=(),
            in_specs=[in_place],
            out_specs=[in_place] * 2,
            scratch_shapes=[
                pltpu.VMEM((slots, edge, edge), jnp.bfloat16),
                pltpu.VMEM((positions, edge, edge), jnp.float32),
                pltpu.VMEM((user_rows, item_rows), jnp.bfloat16),
                pltpu.SemaphoreType.DMA((slots // slot_block,)),
                pltpu.SemaphoreType.DMA((user_tiles,)),
            ],
        ),
        compiler_params=pltpu.CompilerParams(vmem_limit_bytes=24 << 20),
        cost_estimate=pl.CostEstimate(
            flops=4 * slots * edge * edge,
            bytes_accessed=2 * slots * edge * edge + 2 * user_rows * item_rows,
            transcendentals=0,
        ),
        name="dense_block",
    )(row_ids, col_ids, norm_ids, count, in_main(tile_block))


def assemble_kernel(*refs):
    *parts, near, sems = refs
    rows = parts[0].shape[0] // 4
    table = near.shape[0] // 2
    copies = []
    for index, part in enumerate(parts):
        for quarter in range(4):
            side, kind = divmod(quarter, 2)
            place = kind * table + (2 * index + side) * rows
            copies.append(
                pltpu.make_async_copy(
                    part.at[pl.ds(quarter * rows, rows)],
                    near.at[pl.ds(place, rows)],
                    sems.at[4 * index + quarter],
                )
            )
    for copy in copies:
        copy.start()
    for copy in copies:
        copy.wait()


def assemble(parts):
    rows, width = parts[0].shape
    return pl.pallas_call(
        assemble_kernel,
        out_shape=jax.ShapeDtypeStruct((len(parts) * rows, width), parts[0].dtype),
        compiler_params=pltpu.CompilerParams(vmem_limit_bytes=8 << 20),
        scratch_shapes=[pltpu.SemaphoreType.DMA((4 * len(parts),))],
        name="assemble",
    )(*parts)


def lay_out_kernel(grad_user, user_emb, grad_item, item_emb, mine, pair, pieces):
    rows = grad_user.shape[0]
    mine[:rows] = grad_user[...]
    mine[rows:] = user_emb[...]
    pair[:rows] = grad_user[...]
    pair[rows : 2 * rows] = user_emb[...]
    pair[2 * rows :] = jnp.zeros((2 * rows, pair.shape[1]), pair.dtype)
    item_rows = grad_item.shape[0]
    for peer in range(pieces.shape[0]):
        pieces[peer, :item_rows] = grad_item[...]
        pieces[peer, item_rows:] = item_emb[...]


def lay_out(grad_user, user_emb, grad_item, item_emb):
    peers = lax.axis_size("au")
    rows, width = grad_user.shape
    return pl.pallas_call(
        lay_out_kernel,
        out_shape=[
            jax.ShapeDtypeStruct((2 * rows, width), grad_user.dtype),
            jax.ShapeDtypeStruct((4 * rows, width), grad_user.dtype),
            jax.ShapeDtypeStruct((peers, 2 * grad_item.shape[0], width), grad_item.dtype),
        ],
        name="lay_out",
    )(grad_user, user_emb, grad_item, item_emb)


def transposed_product(left, right):
    return lax.dot_general(
        left, right, (((0,), (0,)), ((), ())), preferred_element_type=jnp.float32
    )


def finish_kernel(
    dense_near,
    dense_far,
    item_rows,
    near_in,
    far_in,
    user_near,
    user_far,
    pieces,
    dense,
    sources,
    users,
    q_turned,
    source_sems,
    dense_sems,
    user_sems,
):
    low = jnp.bfloat16
    peers, both_rows, width = item_rows.shape
    piece_rows = both_rows // 2
    half_rows, all_items = dense.shape[1:]
    tiles = half_rows // step
    source_copies = [
        pltpu.make_async_copy(ref, sources.at[half], source_sems.at[half])
        for half, ref in enumerate((near_in, far_in))
    ]
    dense_copies = []
    user_copies = []
    for half in range(2):
        for tile in range(tiles):
            rows = pl.ds(tile * step, step)
            index = half * tiles + tile
            dense_copies.append(
                pltpu.make_async_copy(
                    (dense_near, dense_far)[half].at[rows],
                    dense.at[half, rows],
                    dense_sems.at[index],
                )
            )
            user_copies.append(
                pltpu.make_async_copy(
                    users.at[half, rows],
                    (user_near, user_far)[half].at[rows],
                    user_sems.at[index],
                )
            )
    for half in range(2):
        for copy in dense_copies[half * tiles : (half + 1) * tiles]:
            copy.start()
        source_copies[half].start()
    items = item_rows[:, :piece_rows].reshape(all_items, width)
    weight_term = jnp.zeros((width, width), jnp.float32)
    for half in range(2):
        for tile in range(tiles):
            dense_copies[half * tiles + tile].wait()
            rows = pl.ds(tile * step, step)
            users[half, rows] = jnp.dot(
                dense[half, rows], items, preferred_element_type=jnp.float32
            ).astype(low)
        source_copies[half].wait()
        weight_term += transposed_product(sources[half, half_rows:], users[half])
        for copy in user_copies[half * tiles : (half + 1) * tiles]:
            copy.start()
        turned = sources[half, :half_rows].T
        for start in range(0, all_items, step):
            part = jnp.dot(
                turned, dense[half, :, start : start + step], preferred_element_type=jnp.float32
            )
            if half == 0:
                q_turned[:, start : start + step] = part
            else:
                q_turned[:, start : start + step] += part
    q_low = q_turned[...].astype(low)
    table = item_rows[:, piece_rows:].reshape(all_items, width)
    weight_term += jnp.dot(q_low, table, preferred_element_type=jnp.float32).T
    pieces[:, :piece_rows] = q_turned[...].T.astype(low).reshape(peers, piece_rows, width)
    pieces[:, piece_rows:] = weight_term.reshape(peers, width // peers, width).astype(low)
    for copy in user_copies:
        copy.wait()


def finish(dense_near, dense_far, item_pieces, near, far):
    half_rows, all_items = dense_near.shape
    peers, both_rows, width = item_pieces.shape
    low = jnp.bfloat16
    strip = both_rows // 2 + width // peers
    in_place = pl.BlockSpec(memory_space=pl.ANY)
    in_core = pl.BlockSpec(memory_space=pltpu.VMEM)
    tiles = half_rows // step
    return pl.pallas_call(
        finish_kernel,
        in_specs=[in_place, in_place, in_core, in_place, in_place],
        out_specs=[in_place, in_place, in_core],
        out_shape=[
            jax.ShapeDtypeStruct((half_rows, width), low),
            jax.ShapeDtypeStruct((half_rows, width), low),
            jax.ShapeDtypeStruct((peers, strip, width), low),
        ],
        scratch_shapes=[
            pltpu.VMEM((2, half_rows, all_items), low),
            pltpu.VMEM((2, 2 * half_rows, width), low),
            pltpu.VMEM((2, half_rows, width), low),
            pltpu.VMEM((width, all_items), jnp.float32),
            pltpu.SemaphoreType.DMA((2,)),
            pltpu.SemaphoreType.DMA((2 * tiles,)),
            pltpu.SemaphoreType.DMA((2 * tiles,)),
        ],
        compiler_params=pltpu.CompilerParams(vmem_limit_bytes=32 << 20),
        cost_estimate=pl.CostEstimate(
            flops=8 * half_rows * all_items * width,
            bytes_accessed=4 * half_rows * all_items + 8 * half_rows * width,
            transcendentals=0,
        ),
        name="finish",
    )(in_main(dense_near), in_main(dense_far), item_pieces, in_main(near), in_main(far))


def product(spec, left, right):
    return jnp.einsum(spec, left, right, preferred_element_type=jnp.float32)


def wide(value):
    return value.astype(jnp.float32)


def device_step(
    user_emb,
    item_emb,
    weight,
    grad_user,
    grad_item,
    tile_values,
    tile_rows,
    tile_cols,
    tile_norm,
    tile_count,
):
    width = weight.shape[0]
    user_rows = user_emb.shape[1] * lax.axis_size("ia")
    item_rows = item_emb.shape[1] * lax.axis_size("au")
    low = jnp.bfloat16
    ring = lax.axis_size("ia") // ring_step

    mine, pair, item_sent = lay_out(grad_user[0], user_emb[0], grad_item[0], item_emb[0])
    beside = partner(mine, side_bit)
    pair = lax.dynamic_update_slice(pair, beside, (mine.shape[0], 0))
    own_rows = user_emb.shape[1]
    item_pieces = lax.all_to_all(item_sent, "au", split_axis=0, concat_axis=0, tiled=True)
    parts = [pair]
    for distance in range(1, ring):
        parts.append(from_ahead(pair, distance))
    near = assemble(parts)
    far = partner(near, core_bit)

    dense_near, dense_far = dense_block(
        tile_values[0],
        relative_rows(tile_rows[0]),
        tile_cols[0],
        tile_norm[0],
        tile_count[0],
        user_rows,
        item_rows,
    )
    user_near, user_far, pieces = finish(dense_near, dense_far, item_pieces, near, far)
    peers = lax.axis_size("au")
    arrived = lax.all_to_all(pieces, "au", split_axis=0, concat_axis=0, tiled=True)
    arrived = summed(arrived)
    q_item = arrived[: item_rows // peers]
    strip = summed(from_everyone(arrived[item_rows // peers :].astype(low), "ia"))
    user_count = user_rows * lax.axis_size("au")
    item_count = item_rows * lax.axis_size("ia")
    strip = strip / math.sqrt(user_count + item_count)
    grad_weight = wide(from_everyone(strip.astype(low), "au")).reshape(width, width)

    across = partner(user_far, core_bit)
    along = (wide(user_near) + wide(across)).reshape(ring, user_rows // (2 * ring), width)
    sent = along.astype(low)
    both = along[0] + sum(wide(send_ahead(sent[d], d)) for d in range(1, ring))
    q_user = both[:own_rows] + wide(partner(both[own_rows:].astype(low), side_bit))

    grad_user_emb = product("re,de->rd", q_user.astype(low), weight).astype(low)
    grad_item_emb = product("re,de->rd", q_item.astype(low), weight).astype(low)
    return (grad_user_emb[None], grad_item_emb[None], grad_weight)


def solution(mesh):
    return jax.shard_map(
        device_step,
        mesh=mesh,
        in_specs=(
            P("au", "ia", None),
            P("ia", "au", None),
            P(),
            P("au", "ia", None),
            P("ia", "au", None),
            P("au", "ia", None, None),
            P("au", "ia"),
            P("au", "ia"),
            P("au", "ia"),
            P("au", "ia"),
        ),
        out_specs=(P("au", "ia", None), P("ia", "au", None), P()),
        check_vma=False,
    )
```

```python
import math

import jax
import jax.numpy as jnp
from jax import lax
from jax.experimental import pallas as pl
from jax.experimental.pallas import tpu as pltpu
from jax.sharding import PartitionSpec as P

slot_block = 16
unroll = 4
step = 256
core_bit = 1
side_bit = 2
ring_step = 4


def from_everyone(value, axis):
    copies = jnp.broadcast_to(value, (lax.axis_size(axis), *value.shape))
    return lax.all_to_all(copies, axis, split_axis=0, concat_axis=0, tiled=True)


def partner(value, bit):
    return lax.ppermute(value, "ia", [(i, i ^ bit) for i in range(lax.axis_size("ia"))])


def ahead(index, distance):
    ring = lax.axis_size("ia") // ring_step
    return (index // ring_step + distance) % ring * ring_step + index % ring_step


def from_ahead(value, distance):
    size = lax.axis_size("ia")
    return lax.ppermute(value, "ia", [(ahead(i, distance), i) for i in range(size)])


def send_ahead(value, distance):
    size = lax.axis_size("ia")
    return lax.ppermute(value, "ia", [(i, ahead(i, distance)) for i in range(size)])


def relative_rows(row_ids):
    ring = lax.axis_size("ia") // ring_step
    here = lax.axis_index("ia").astype(jnp.int32)
    core = (row_ids ^ here) & 1
    side = ((row_ids ^ here) >> 1) & 1
    along = ((row_ids >> 2) - (here >> 2)) & (ring - 1)
    return core * (2 * ring) + along * 2 + side


def summed(pieces):
    return pieces.astype(jnp.float32).sum(axis=0)


def in_main(value):
    return pltpu.with_memory_space_constraint(value, pltpu.HBM)


def dense_kernel(
    rows, cols, norms, count, tiles_in, near, far, tiles, total, low, in_sems, out_sems
):
    edge = tiles.shape[1]
    item_tiles = near.shape[1] // edge
    half_tiles = near.shape[0] // edge
    chunks = (count[0] + slot_block - 1) // slot_block

    def chunk_copy(chunk):
        slots = pl.ds(chunk * slot_block, slot_block)
        return pltpu.make_async_copy(tiles_in.at[slots], tiles.at[slots], in_sems.at[chunk])

    def fetch(chunk, carry):
        chunk_copy(chunk).start()
        return carry

    lax.fori_loop(0, chunks, fetch, 0)

    def clear(index, carry):
        total[pl.ds(index * 4, 4)] = jnp.zeros((4, edge, edge), jnp.float32)
        return carry

    lax.fori_loop(0, total.shape[0] // 4, clear, 0)

    def add_chunk(chunk, carry):
        chunk_copy(chunk).wait()

        def add_group(group, inner):
            for lane in range(unroll):
                slot = chunk * slot_block + group * unroll + lane
                place = rows[slot] * item_tiles + cols[slot]
                norm = jnp.full((8, edge), norms[slot], jnp.int32).astype(jnp.float32)
                scale = jnp.where(slot < count[0], 1.0 / norm, 0.0)
                term = tiles[slot].astype(jnp.float32).reshape(edge // 8, 8, edge) * scale[None]
                total[place] = total[place] + term.reshape(edge, edge)
            return inner

        return lax.fori_loop(0, slot_block // unroll, add_group, carry)

    lax.fori_loop(0, chunks, add_chunk, 0)

    def row_copy(half, row):
        kept = pl.ds(pl.multiple_of((half * half_tiles + row) * edge, edge), edge)
        out = pl.ds(pl.multiple_of(row * edge, edge), edge)
        dense = near if half == 0 else far
        return pltpu.make_async_copy(
            low.at[kept], dense.at[out], out_sems.at[half * half_tiles + row]
        )

    for half in range(2):

        def finish_row(row, carry):
            start = pl.multiple_of((half * half_tiles + row) * edge, edge)
            for col in range(item_tiles):
                low[pl.ds(start, edge), col * edge : (col + 1) * edge] = total[
                    (half * half_tiles + row) * item_tiles + col
                ].astype(jnp.bfloat16)

            @pl.when(row > 0)
            def send():
                row_copy(half, row - 1).start()

            return carry

        lax.fori_loop(0, half_tiles, finish_row, 0)
        if half == 1:
            row_copy(0, half_tiles - 1).start()
    row_copy(1, half_tiles - 1).start()
    for half in range(2):

        def wait_row(row, carry):
            row_copy(half, row).wait()
            return carry

        lax.fori_loop(0, half_tiles, wait_row, 0)


def dense_block(tile_block, row_ids, col_ids, norm_ids, count, user_rows, item_rows):
    slots, edge, _ = tile_block.shape
    user_tiles = user_rows // edge
    positions = user_tiles * (item_rows // edge)
    in_place = pl.BlockSpec(memory_space=pltpu.HBM)
    return pl.pallas_call(
        dense_kernel,
        out_shape=[pltpu.HBM((user_rows // 2, item_rows), jnp.bfloat16)] * 2,
        grid_spec=pltpu.PrefetchScalarGridSpec(
            num_scalar_prefetch=4,
            grid=(),
            in_specs=[in_place],
            out_specs=[in_place] * 2,
            scratch_shapes=[
                pltpu.VMEM((slots, edge, edge), jnp.bfloat16),
                pltpu.VMEM((positions, edge, edge), jnp.float32),
                pltpu.VMEM((user_rows, item_rows), jnp.bfloat16),
                pltpu.SemaphoreType.DMA((slots // slot_block,)),
                pltpu.SemaphoreType.DMA((user_tiles,)),
            ],
        ),
        compiler_params=pltpu.CompilerParams(vmem_limit_bytes=24 << 20),
        cost_estimate=pl.CostEstimate(
            flops=4 * slots * edge * edge,
            bytes_accessed=2 * slots * edge * edge + 2 * user_rows * item_rows,
            transcendentals=0,
        ),
        name="dense_block",
    )(row_ids, col_ids, norm_ids, count, in_main(tile_block))


def assemble_kernel(*refs):
    *parts, near, sems = refs
    rows = parts[0].shape[0] // 4
    table = near.shape[0] // 2
    copies = []
    for index, part in enumerate(parts):
        for quarter in range(4):
            side, kind = divmod(quarter, 2)
            place = kind * table + (2 * index + side) * rows
            copies.append(
                pltpu.make_async_copy(
                    part.at[pl.ds(quarter * rows, rows)],
                    near.at[pl.ds(place, rows)],
                    sems.at[4 * index + quarter],
                )
            )
    for copy in copies:
        copy.start()
    for copy in copies:
        copy.wait()


def assemble(parts):
    rows, width = parts[0].shape
    return pl.pallas_call(
        assemble_kernel,
        out_shape=jax.ShapeDtypeStruct((len(parts) * rows, width), parts[0].dtype),
        compiler_params=pltpu.CompilerParams(vmem_limit_bytes=8 << 20),
        scratch_shapes=[pltpu.SemaphoreType.DMA((4 * len(parts),))],
        name="assemble",
    )(*parts)


def lay_out_kernel(grad_user, user_emb, grad_item, item_emb, mine, pair, pieces, sems):
    rows = grad_user.shape[0]
    item_rows = grad_item.shape[0]
    moves = []
    for index, source in enumerate((grad_user, user_emb)):
        for target in (mine, pair):
            moves.append((source, target.at[pl.ds(index * rows, rows)]))
    moves.append((grad_user, pair.at[pl.ds(2 * rows, rows)]))
    moves.append((user_emb, pair.at[pl.ds(3 * rows, rows)]))
    for peer in range(pieces.shape[0]):
        for index, source in enumerate((grad_item, item_emb)):
            moves.append((source, pieces.at[peer, pl.ds(index * item_rows, item_rows)]))
    copies = [
        pltpu.make_async_copy(source, target, sems.at[index])
        for index, (source, target) in enumerate(moves)
    ]
    for copy in copies:
        copy.start()
    for copy in copies:
        copy.wait()


def lay_out(grad_user, user_emb, grad_item, item_emb):
    peers = lax.axis_size("au")
    rows, width = grad_user.shape
    in_place = pl.BlockSpec(memory_space=pltpu.HBM)
    return pl.pallas_call(
        lay_out_kernel,
        out_specs=[in_place] * 3,
        out_shape=[
            jax.ShapeDtypeStruct((2 * rows, width), grad_user.dtype),
            jax.ShapeDtypeStruct((4 * rows, width), grad_user.dtype),
            jax.ShapeDtypeStruct((peers, 2 * grad_item.shape[0], width), grad_item.dtype),
        ],
        scratch_shapes=[pltpu.SemaphoreType.DMA((6 + 2 * peers,))],
        name="lay_out",
    )(grad_user, user_emb, grad_item, item_emb)


def transposed_product(left, right):
    return lax.dot_general(
        left, right, (((0,), (0,)), ((), ())), preferred_element_type=jnp.float32
    )


def finish_kernel(
    dense_near,
    dense_far,
    item_rows,
    near_in,
    far_in,
    user_near,
    user_far,
    pieces,
    dense,
    sources,
    q_turned,
    sems,
):
    low = jnp.bfloat16
    peers, both_rows, width = item_rows.shape
    piece_rows = both_rows // 2
    half_rows, all_items = dense.shape[1:]
    dense_copies = [
        pltpu.make_async_copy(ref, dense.at[half], sems.at[half])
        for half, ref in enumerate((dense_near, dense_far))
    ]
    source_copies = [
        pltpu.make_async_copy(ref, sources.at[half], sems.at[2 + half])
        for half, ref in enumerate((near_in, far_in))
    ]
    for half in range(2):
        dense_copies[half].start()
        source_copies[half].start()
    items = item_rows[:, :piece_rows].reshape(all_items, width)
    weight_term = jnp.zeros((width, width), jnp.float32)
    for half, user in enumerate((user_near, user_far)):
        dense_copies[half].wait()
        for start in range(0, half_rows, step):
            rows = dense[half, start : start + step]
            user[start : start + step] = jnp.dot(
                rows, items, preferred_element_type=jnp.float32
            ).astype(low)
        source_copies[half].wait()
        weight_term += transposed_product(sources[half, half_rows:], user[...])
        turned = sources[half, :half_rows].T
        for start in range(0, all_items, step):
            part = jnp.dot(
                turned, dense[half, :, start : start + step], preferred_element_type=jnp.float32
            )
            if half == 0:
                q_turned[:, start : start + step] = part
            else:
                q_turned[:, start : start + step] += part
    q_low = q_turned[...].astype(low)
    table = item_rows[:, piece_rows:].reshape(all_items, width)
    weight_term += jnp.dot(q_low, table, preferred_element_type=jnp.float32).T
    pieces[:, :piece_rows] = q_turned[...].T.astype(low).reshape(peers, piece_rows, width)
    pieces[:, piece_rows:] = weight_term.reshape(peers, width // peers, width).astype(low)


def finish(dense_near, dense_far, item_pieces, near, far):
    half_rows, all_items = dense_near.shape
    peers, both_rows, width = item_pieces.shape
    low = jnp.bfloat16
    strip = both_rows // 2 + width // peers
    in_place = pl.BlockSpec(memory_space=pltpu.HBM)
    in_core = pl.BlockSpec(memory_space=pltpu.VMEM)
    return pl.pallas_call(
        finish_kernel,
        in_specs=[in_place, in_place, in_core, in_place, in_place],
        out_shape=[
            jax.ShapeDtypeStruct((half_rows, width), low),
            jax.ShapeDtypeStruct((half_rows, width), low),
            jax.ShapeDtypeStruct((peers, strip, width), low),
        ],
        scratch_shapes=[
            pltpu.VMEM((2, half_rows, all_items), low),
            pltpu.VMEM((2, 2 * half_rows, width), low),
            pltpu.VMEM((width, all_items), jnp.float32),
            pltpu.SemaphoreType.DMA((4,)),
        ],
        compiler_params=pltpu.CompilerParams(vmem_limit_bytes=32 << 20),
        cost_estimate=pl.CostEstimate(
            flops=8 * half_rows * all_items * width,
            bytes_accessed=4 * half_rows * all_items + 8 * half_rows * width,
            transcendentals=0,
        ),
        name="finish",
    )(in_main(dense_near), in_main(dense_far), item_pieces, in_main(near), in_main(far))


def product(spec, left, right):
    return jnp.einsum(spec, left, right, preferred_element_type=jnp.float32)


def wide(value):
    return value.astype(jnp.float32)


def device_step(
    user_emb,
    item_emb,
    weight,
    grad_user,
    grad_item,
    tile_values,
    tile_rows,
    tile_cols,
    tile_norm,
    tile_count,
):
    width = weight.shape[0]
    user_rows = user_emb.shape[1] * lax.axis_size("ia")
    item_rows = item_emb.shape[1] * lax.axis_size("au")
    low = jnp.bfloat16
    ring = lax.axis_size("ia") // ring_step

    mine, pair, item_sent = lay_out(grad_user[0], user_emb[0], grad_item[0], item_emb[0])
    beside = partner(mine, side_bit)
    pair = lax.dynamic_update_slice(pair, beside, (mine.shape[0], 0))
    own_rows = user_emb.shape[1]
    item_pieces = lax.all_to_all(item_sent, "au", split_axis=0, concat_axis=0, tiled=True)
    parts = [pair]
    for distance in range(1, ring):
        parts.append(from_ahead(pair, distance))
    near = assemble(parts)
    far = partner(near, core_bit)

    dense_near, dense_far = dense_block(
        tile_values[0],
        relative_rows(tile_rows[0]),
        tile_cols[0],
        tile_norm[0],
        tile_count[0],
        user_rows,
        item_rows,
    )
    user_near, user_far, pieces = finish(dense_near, dense_far, item_pieces, near, far)
    peers = lax.axis_size("au")
    arrived = lax.all_to_all(pieces, "au", split_axis=0, concat_axis=0, tiled=True)
    arrived = summed(arrived)
    q_item = arrived[: item_rows // peers]
    strip = summed(from_everyone(arrived[item_rows // peers :].astype(low), "ia"))
    user_count = user_rows * lax.axis_size("au")
    item_count = item_rows * lax.axis_size("ia")
    strip = strip / math.sqrt(user_count + item_count)
    grad_weight = wide(from_everyone(strip.astype(low), "au")).reshape(width, width)

    across = partner(user_far, core_bit)
    along = (wide(user_near) + wide(across)).reshape(ring, user_rows // (2 * ring), width)
    sent = along.astype(low)
    both = along[0] + sum(wide(send_ahead(sent[d], d)) for d in range(1, ring))
    q_user = both[:own_rows] + wide(partner(both[own_rows:].astype(low), side_bit))

    grad_user_emb = product("re,de->rd", q_user.astype(low), weight).astype(low)
    grad_item_emb = product("re,de->rd", q_item.astype(low), weight).astype(low)
    return (grad_user_emb[None], grad_item_emb[None], grad_weight)


def solution(mesh):
    return jax.shard_map(
        device_step,
        mesh=mesh,
        in_specs=(
            P("au", "ia", None),
            P("ia", "au", None),
            P(),
            P("au", "ia", None),
            P("ia", "au", None),
            P("au", "ia", None, None),
            P("au", "ia"),
            P("au", "ia"),
            P("au", "ia"),
            P("au", "ia"),
        ),
        out_specs=(P("au", "ia", None), P("ia", "au", None), P()),
        check_vma=False,
    )
```

```python
import math

import jax
import jax.numpy as jnp
from jax import lax
from jax.experimental import pallas as pl
from jax.experimental.pallas import tpu as pltpu
from jax.sharding import PartitionSpec as P

slot_block = 16
unroll = 4
step = 256
core_bit = 1
side_bit = 2
ring_step = 4


def from_everyone(value, axis):
    copies = jnp.broadcast_to(value, (lax.axis_size(axis), *value.shape))
    return lax.all_to_all(copies, axis, split_axis=0, concat_axis=0, tiled=True)


def partner(value, bit):
    return lax.ppermute(value, "ia", [(i, i ^ bit) for i in range(lax.axis_size("ia"))])


def ahead(index, distance):
    ring = lax.axis_size("ia") // ring_step
    return (index // ring_step + distance) % ring * ring_step + index % ring_step


def from_ahead(value, distance):
    size = lax.axis_size("ia")
    return lax.ppermute(value, "ia", [(ahead(i, distance), i) for i in range(size)])


def send_ahead(value, distance):
    size = lax.axis_size("ia")
    return lax.ppermute(value, "ia", [(i, ahead(i, distance)) for i in range(size)])


def relative_rows(row_ids):
    ring = lax.axis_size("ia") // ring_step
    here = lax.axis_index("ia").astype(jnp.int32)
    core = (row_ids ^ here) & 1
    side = ((row_ids ^ here) >> 1) & 1
    along = ((row_ids >> 2) - (here >> 2)) & (ring - 1)
    return core * (2 * ring) + along * 2 + side


def summed(pieces):
    return pieces.astype(jnp.float32).sum(axis=0)


def in_main(value):
    return pltpu.with_memory_space_constraint(value, pltpu.HBM)


def dense_kernel(
    rows, cols, norms, count, tiles_in, near, far, tiles, total, low, in_sems, out_sems
):
    edge = tiles.shape[1]
    item_tiles = near.shape[1] // edge
    half_tiles = near.shape[0] // edge
    chunks = (count[0] + slot_block - 1) // slot_block

    def chunk_copy(chunk):
        slots = pl.ds(chunk * slot_block, slot_block)
        return pltpu.make_async_copy(tiles_in.at[slots], tiles.at[slots], in_sems.at[chunk])

    def fetch(chunk, carry):
        chunk_copy(chunk).start()
        return carry

    lax.fori_loop(0, chunks, fetch, 0)

    def clear(index, carry):
        total[pl.ds(index * 4, 4)] = jnp.zeros((4, edge, edge), jnp.float32)
        return carry

    lax.fori_loop(0, total.shape[0] // 4, clear, 0)

    def add_chunk(chunk, carry):
        chunk_copy(chunk).wait()

        def add_group(group, inner):
            for lane in range(unroll):
                slot = chunk * slot_block + group * unroll + lane
                place = rows[slot] * item_tiles + cols[slot]
                norm = jnp.full((8, edge), norms[slot], jnp.int32).astype(jnp.float32)
                scale = jnp.where(slot < count[0], 1.0 / norm, 0.0)
                term = tiles[slot].astype(jnp.float32).reshape(edge // 8, 8, edge) * scale[None]
                total[place] = total[place] + term.reshape(edge, edge)
            return inner

        return lax.fori_loop(0, slot_block // unroll, add_group, carry)

    lax.fori_loop(0, chunks, add_chunk, 0)

    def row_copy(half, row):
        kept = pl.ds(pl.multiple_of((half * half_tiles + row) * edge, edge), edge)
        out = pl.ds(pl.multiple_of(row * edge, edge), edge)
        dense = near if half == 0 else far
        return pltpu.make_async_copy(
            low.at[kept], dense.at[out], out_sems.at[half * half_tiles + row]
        )

    for half in range(2):

        def finish_row(row, carry):
            start = pl.multiple_of((half * half_tiles + row) * edge, edge)
            for col in range(item_tiles):
                low[pl.ds(start, edge), col * edge : (col + 1) * edge] = total[
                    (half * half_tiles + row) * item_tiles + col
                ].astype(jnp.bfloat16)

            @pl.when(row > 0)
            def send():
                row_copy(half, row - 1).start()

            return carry

        lax.fori_loop(0, half_tiles, finish_row, 0)
        if half == 1:
            row_copy(0, half_tiles - 1).start()
    row_copy(1, half_tiles - 1).start()
    for half in range(2):

        def wait_row(row, carry):
            row_copy(half, row).wait()
            return carry

        lax.fori_loop(0, half_tiles, wait_row, 0)


def dense_block(tile_block, row_ids, col_ids, norm_ids, count, user_rows, item_rows):
    slots, edge, _ = tile_block.shape
    user_tiles = user_rows // edge
    positions = user_tiles * (item_rows // edge)
    in_place = pl.BlockSpec(memory_space=pltpu.HBM)
    return pl.pallas_call(
        dense_kernel,
        out_shape=[pltpu.HBM((user_rows // 2, item_rows), jnp.bfloat16)] * 2,
        grid_spec=pltpu.PrefetchScalarGridSpec(
            num_scalar_prefetch=4,
            grid=(),
            in_specs=[in_place],
            out_specs=[in_place] * 2,
            scratch_shapes=[
                pltpu.VMEM((slots, edge, edge), jnp.bfloat16),
                pltpu.VMEM((positions, edge, edge), jnp.float32),
                pltpu.VMEM((user_rows, item_rows), jnp.bfloat16),
                pltpu.SemaphoreType.DMA((slots // slot_block,)),
                pltpu.SemaphoreType.DMA((user_tiles,)),
            ],
        ),
        compiler_params=pltpu.CompilerParams(vmem_limit_bytes=24 << 20),
        cost_estimate=pl.CostEstimate(
            flops=4 * slots * edge * edge,
            bytes_accessed=2 * slots * edge * edge + 2 * user_rows * item_rows,
            transcendentals=0,
        ),
        name="dense_block",
    )(row_ids, col_ids, norm_ids, count, in_main(tile_block))


def assemble_kernel(*refs):
    *parts, near, sems = refs
    rows = parts[0].shape[0] // 4
    table = near.shape[0] // 2
    copies = []
    for index, part in enumerate(parts):
        for quarter in range(4):
            side, kind = divmod(quarter, 2)
            place = kind * table + (2 * index + side) * rows
            copies.append(
                pltpu.make_async_copy(
                    part.at[pl.ds(quarter * rows, rows)],
                    near.at[pl.ds(place, rows)],
                    sems.at[4 * index + quarter],
                )
            )
    for copy in copies:
        copy.start()
    for copy in copies:
        copy.wait()


def assemble(parts):
    rows, width = parts[0].shape
    return pl.pallas_call(
        assemble_kernel,
        out_shape=jax.ShapeDtypeStruct((len(parts) * rows, width), parts[0].dtype),
        compiler_params=pltpu.CompilerParams(vmem_limit_bytes=8 << 20),
        scratch_shapes=[pltpu.SemaphoreType.DMA((4 * len(parts),))],
        name="assemble",
    )(*parts)


def lay_out_kernel(grad_user, user_emb, grad_item, item_emb, mine, pair, pieces):
    rows = grad_user.shape[0]
    mine[:rows] = grad_user[...]
    mine[rows:] = user_emb[...]
    pair[:rows] = grad_user[...]
    pair[rows : 2 * rows] = user_emb[...]
    pair[2 * rows :] = jnp.zeros((2 * rows, pair.shape[1]), pair.dtype)
    item_rows = grad_item.shape[0]
    for peer in range(pieces.shape[0]):
        pieces[peer, :item_rows] = grad_item[...]
        pieces[peer, item_rows:] = item_emb[...]


def lay_out(grad_user, user_emb, grad_item, item_emb):
    peers = lax.axis_size("au")
    rows, width = grad_user.shape
    return pl.pallas_call(
        lay_out_kernel,
        out_shape=[
            jax.ShapeDtypeStruct((2 * rows, width), grad_user.dtype),
            jax.ShapeDtypeStruct((4 * rows, width), grad_user.dtype),
            jax.ShapeDtypeStruct((peers, 2 * grad_item.shape[0], width), grad_item.dtype),
        ],
        name="lay_out",
    )(grad_user, user_emb, grad_item, item_emb)


def transposed_product(left, right):
    return lax.dot_general(
        left, right, (((0,), (0,)), ((), ())), preferred_element_type=jnp.float32
    )


def finish_kernel(
    dense_near,
    dense_far,
    item_rows,
    near_in,
    far_in,
    user_near,
    user_far,
    pieces,
    dense,
    sources,
    q_turned,
    sems,
):
    low = jnp.bfloat16
    peers, both_rows, width = item_rows.shape
    piece_rows = both_rows // 2
    half_rows, all_items = dense.shape[1:]
    split = half_rows // 2
    first = [
        pltpu.make_async_copy(
            dense_near.at[pl.ds(start, split)], dense.at[0, pl.ds(start, split)], sems.at[index]
        )
        for start, index in ((0, 0), (split, 4))
    ]
    far_copy = pltpu.make_async_copy(dense_far, dense.at[1], sems.at[1])
    source_copies = [
        pltpu.make_async_copy(ref, sources.at[half], sems.at[2 + half])
        for half, ref in enumerate((near_in, far_in))
    ]
    for copy in (*first, source_copies[0], far_copy, source_copies[1]):
        copy.start()
    items = item_rows[:, :piece_rows].reshape(all_items, width)
    weight_term = jnp.zeros((width, width), jnp.float32)
    for half, user in enumerate((user_near, user_far)):
        if half == 1:
            far_copy.wait()
        for start in range(0, half_rows, step):
            if half == 0 and start % split == 0:
                first[start // split].wait()
            rows = dense[half, start : start + step]
            user[start : start + step] = jnp.dot(
                rows, items, preferred_element_type=jnp.float32
            ).astype(low)
        source_copies[half].wait()
        weight_term += transposed_product(sources[half, half_rows:], user[...])
        turned = sources[half, :half_rows].T
        for start in range(0, all_items, step):
            part = jnp.dot(
                turned, dense[half, :, start : start + step], preferred_element_type=jnp.float32
            )
            if half == 0:
                q_turned[:, start : start + step] = part
            else:
                q_turned[:, start : start + step] += part
    q_low = q_turned[...].astype(low)
    table = item_rows[:, piece_rows:].reshape(all_items, width)
    weight_term += jnp.dot(q_low, table, preferred_element_type=jnp.float32).T
    pieces[:, :piece_rows] = q_turned[...].T.astype(low).reshape(peers, piece_rows, width)
    pieces[:, piece_rows:] = weight_term.reshape(peers, width // peers, width).astype(low)


def finish(dense_near, dense_far, item_pieces, near, far):
    half_rows, all_items = dense_near.shape
    peers, both_rows, width = item_pieces.shape
    low = jnp.bfloat16
    strip = both_rows // 2 + width // peers
    in_place = pl.BlockSpec(memory_space=pltpu.HBM)
    in_core = pl.BlockSpec(memory_space=pltpu.VMEM)
    return pl.pallas_call(
        finish_kernel,
        in_specs=[in_place, in_place, in_core, in_place, in_place],
        out_shape=[
            jax.ShapeDtypeStruct((half_rows, width), low),
            jax.ShapeDtypeStruct((half_rows, width), low),
            jax.ShapeDtypeStruct((peers, strip, width), low),
        ],
        scratch_shapes=[
            pltpu.VMEM((2, half_rows, all_items), low),
            pltpu.VMEM((2, 2 * half_rows, width), low),
            pltpu.VMEM((width, all_items), jnp.float32),
            pltpu.SemaphoreType.DMA((5,)),
        ],
        compiler_params=pltpu.CompilerParams(vmem_limit_bytes=32 << 20),
        cost_estimate=pl.CostEstimate(
            flops=8 * half_rows * all_items * width,
            bytes_accessed=4 * half_rows * all_items + 8 * half_rows * width,
            transcendentals=0,
        ),
        name="finish",
    )(in_main(dense_near), in_main(dense_far), item_pieces, in_main(near), in_main(far))


def product(spec, left, right):
    return jnp.einsum(spec, left, right, preferred_element_type=jnp.float32)


def wide(value):
    return value.astype(jnp.float32)


def device_step(
    user_emb,
    item_emb,
    weight,
    grad_user,
    grad_item,
    tile_values,
    tile_rows,
    tile_cols,
    tile_norm,
    tile_count,
):
    width = weight.shape[0]
    user_rows = user_emb.shape[1] * lax.axis_size("ia")
    item_rows = item_emb.shape[1] * lax.axis_size("au")
    low = jnp.bfloat16
    ring = lax.axis_size("ia") // ring_step

    mine, pair, item_sent = lay_out(grad_user[0], user_emb[0], grad_item[0], item_emb[0])
    beside = partner(mine, side_bit)
    pair = lax.dynamic_update_slice(pair, beside, (mine.shape[0], 0))
    own_rows = user_emb.shape[1]
    item_pieces = lax.all_to_all(item_sent, "au", split_axis=0, concat_axis=0, tiled=True)
    parts = [pair]
    for distance in range(1, ring):
        parts.append(from_ahead(pair, distance))
    near = assemble(parts)
    far = partner(near, core_bit)

    dense_near, dense_far = dense_block(
        tile_values[0],
        relative_rows(tile_rows[0]),
        tile_cols[0],
        tile_norm[0],
        tile_count[0],
        user_rows,
        item_rows,
    )
    user_near, user_far, pieces = finish(dense_near, dense_far, item_pieces, near, far)
    peers = lax.axis_size("au")
    arrived = lax.all_to_all(pieces, "au", split_axis=0, concat_axis=0, tiled=True)
    arrived = summed(arrived)
    q_item = arrived[: item_rows // peers]
    strip = summed(from_everyone(arrived[item_rows // peers :].astype(low), "ia"))
    user_count = user_rows * lax.axis_size("au")
    item_count = item_rows * lax.axis_size("ia")
    strip = strip / math.sqrt(user_count + item_count)
    grad_weight = wide(from_everyone(strip.astype(low), "au")).reshape(width, width)

    across = partner(user_far, core_bit)
    along = (wide(user_near) + wide(across)).reshape(ring, user_rows // (2 * ring), width)
    sent = along.astype(low)
    both = along[0] + sum(wide(send_ahead(sent[d], d)) for d in range(1, ring))
    q_user = both[:own_rows] + wide(partner(both[own_rows:].astype(low), side_bit))

    grad_user_emb = product("re,de->rd", q_user.astype(low), weight).astype(low)
    grad_item_emb = product("re,de->rd", q_item.astype(low), weight).astype(low)
    return (grad_user_emb[None], grad_item_emb[None], grad_weight)


def solution(mesh):
    return jax.shard_map(
        device_step,
        mesh=mesh,
        in_specs=(
            P("au", "ia", None),
            P("ia", "au", None),
            P(),
            P("au", "ia", None),
            P("ia", "au", None),
            P("au", "ia", None, None),
            P("au", "ia"),
            P("au", "ia"),
            P("au", "ia"),
            P("au", "ia"),
        ),
        out_specs=(P("au", "ia", None), P("ia", "au", None), P()),
        check_vma=False,
    )
```
